32 devices in a mesh: grp: 4 (over x, core), seq: 8 (over z, y).
Axes of the slice: x: 2, y: 2, z: 4, core: 2. Of those that a mesh axis runs over, the one named last changes fastest.
Arguments:
- tokens: bfloat16 [32, 64, 128, 512], P(None, 'grp', 'seq'), may hold values from -6 to 6
- cotangent: bfloat16 [32, 64, 128, 512], P(None, 'grp', 'seq'), may hold values from -6 to 6
- gate_weight: bfloat16 [512, 512], replicated, may hold values from -0.25 to 0.25
- first_factor: bfloat16 [4, 32, 32], replicated, may hold values from -1 to 1
- middle_factor: bfloat16 [4, 64, 64], replicated, may hold values from -0.75 to 0.75
- last_factor: bfloat16 [4, 128, 128], replicated, may hold values from -0.5 to 0.5
Outputs:
- d_tokens: bfloat16 [32, 64, 128, 512], P(None, 'grp', 'seq')
- grad_gate: float32 [512, 512], P('seq')
- grad_first: float32 [4, 32, 32], replicated
- grad_middle: float32 [4, 64, 64], P(None, 'grp')
- grad_last: float32 [4, 128, 128], P(None, 'seq')
The draws below stay inside these ranges and needn't reach their ends.
All inputs are finite; a program needn't handle non-finite values.
Results may differ from the reference program's by a relative error of at most 0.0065.
Values may be sent and summed in bfloat16 or wider, within the bound.
No kernel may reach another device: no remote copies, remote signals or barrier semaphores. Data moves between devices by JAX's collectives and lax.ppermute only.
A program may use at most 192 MiB of HBM per device.

```python
import math
import jax
import jax.numpy as jnp
from jax import lax

F1 = 32
F2 = 64
F3 = 128
D = 512
HEADS = 4
TOKENS = 262144


def spiked(values, stream_key, source, target, parts, factor):
    owner, partner = [(jnp.arange(values.shape[position]) // (values.shape[position] // parts)).reshape([-1 if axis == position else 1 for axis in range(values.ndim)]) for position in (source, target)]
    chosen = jax.random.permutation(stream_key, parts)[partner]
    strong = (owner == chosen) | (owner == (partner + parts // 2) % parts)
    return jnp.where(strong, factor * values, values)


def level_of(key, dims, cuts, low, top_value):
    def one(position, shards_of):
        draws = jax.random.uniform(jax.random.fold_in(jax.random.fold_in(key, 6), position), (shards_of,), jnp.float32, low / len(cuts), top_value / len(cuts))
        return jnp.repeat(jnp.exp(draws), dims[position] // shards_of).reshape((-1,) + (1,) * (len(dims) - position - 1))

    level = one(*cuts[0])
    for cut in cuts[1:]:
        level = level * one(*cut)
    return level


def bell_draw(rng, extent, width, reach, split=(), held_as=jnp.bfloat16):
    factor_of = level_of(rng, extent, split, -0.22, 0.18) if split else 1.0
    values = jax.random.normal(rng, extent, jnp.float32) * width * factor_of
    return jnp.minimum(jnp.maximum(values, -reach), reach).astype(held_as)


def heavy_noise(rng, dims, spread, bound, shards, heavy, held_as=jnp.bfloat16):
    values = spread * jax.random.normal(rng, dims, jnp.float32)
    if shards:
        values = values * level_of(rng, dims, shards, -0.22, 0.18)
    return jnp.clip(spiked(values, jax.random.fold_in(rng, 3), *heavy), -bound, bound).astype(held_as)


def setup_inputs(seed: int = 0) -> dict:
    key_list = jax.random.split(jax.random.key(seed), 7)
    return {
        "tokens": heavy_noise(key_list[0], (F1, F2, F3, D), 1.0, 6.0, ((1, 4), (2, 8)), (2, 3, 8, 2.0)),
        "cotangent": heavy_noise(key_list[1], (F1, F2, F3, D), 1.0, 6.0, ((1, 4), (2, 8)), (1, 3, 4, 2.0)),
        "gate_weight": bell_draw(key_list[2], (D, D), D ** -0.5, 0.25),
        "first_factor": bell_draw(key_list[3], (HEADS, F1, F1), F1 ** -0.5, 1.0),
        "middle_factor": bell_draw(key_list[4], (HEADS, F2, F2), F2 ** -0.5, 0.75),
        "last_factor": bell_draw(key_list[5], (HEADS, F3, F3), F3 ** -0.5, 0.5),
    }


def headed(values):
    return values.reshape(values.shape[:-1] + (HEADS, values.shape[-1] // HEADS))

def mixing(weights, values, form):
    result = jnp.einsum(form, weights.astype(jnp.float32), headed(values).astype(jnp.float32), precision=lax.Precision.HIGHEST)
    return result.reshape(values.shape)

def contract(left, right, form):
    return jnp.einsum(form, headed(left).astype(jnp.float32), headed(right).astype(jnp.float32), precision=lax.Precision.HIGHEST)

def reference(tokens, cotangent, gate_weight, first_factor, middle_factor, last_factor):
    rows = tokens.reshape(-1, D)
    gate = jax.nn.sigmoid(jnp.dot(rows, gate_weight, preferred_element_type=jnp.float32)).reshape(tokens.shape)
    first_out = mixing(first_factor, tokens, 'hab,bjkhe->ajkhe').astype(jnp.bfloat16)
    last_out = mixing(last_factor, first_out, 'hab,ijbhe->ijahe').astype(jnp.bfloat16)
    mixer = mixing(middle_factor, last_out, 'hab,ibkhe->iakhe').astype(jnp.bfloat16)
    upstream = cotangent.astype(jnp.float32)
    d_mix = (upstream * gate).astype(jnp.bfloat16)
    d_pre = (upstream * mixer.astype(jnp.float32) * gate * (1.0 - gate)).astype(jnp.bfloat16)
    middle_back = mixing(middle_factor, d_mix, 'hba,ibkhe->iakhe').astype(jnp.bfloat16)
    last_back = mixing(last_factor, middle_back, 'hba,ijbhe->ijahe').astype(jnp.bfloat16)
    first_back = mixing(first_factor, last_back, 'hba,bjkhe->ajkhe')
    pre_rows = d_pre.reshape(-1, D)
    d_tokens = (first_back.reshape(-1, D) + jnp.dot(pre_rows, gate_weight.T, preferred_element_type=jnp.float32)).astype(jnp.bfloat16).reshape(tokens.shape)
    factor = 1.0 / math.sqrt(TOKENS)
    grad_gate = jnp.dot(rows.T, pre_rows, preferred_element_type=jnp.float32) * factor
    grad_middle = contract(d_mix, last_out, 'iakhe,ibkhe->hab') * factor
    grad_last = contract(middle_back, first_out, 'ijahe,ijbhe->hab') * factor
    grad_first = contract(last_back, tokens, 'ajkhe,bjkhe->hab') * factor
    return (d_tokens, grad_gate, grad_first, grad_middle, grad_last)
```

```python
import functools
import math

import jax
import jax.numpy as jnp
from jax import lax
from jax.experimental import pallas as pl
from jax.experimental.pallas import tpu as pltpu
from jax.sharding import PartitionSpec as P

HEADS = 4
ALL = ("grp", "seq")
F32 = jnp.float32
BF16 = jnp.bfloat16


def headed(values):
    return values.reshape(values.shape[:-1] + (HEADS, values.shape[-1] // HEADS))


def mixing(weights, values, form):
    result = jnp.einsum(form, weights, headed(values), preferred_element_type=F32)
    return result.reshape(values.shape)


def contract(left, right, form):
    return jnp.einsum(form, headed(left), headed(right), preferred_element_type=F32)


def send_last(values):
    return lax.all_to_all(values, "seq", split_axis=0, concat_axis=2, tiled=True)


def send_middle(values):
    return lax.all_to_all(values, "grp", split_axis=2, concat_axis=1, tiled=True)


def return_middle(values):
    return lax.all_to_all(values, "grp", split_axis=1, concat_axis=2, tiled=True)


def return_last(values):
    return lax.all_to_all(values, "seq", split_axis=2, concat_axis=0, tiled=True)


def positions(tokens):
    return math.prod(tokens.shape[:3]) * lax.axis_size("grp") * lax.axis_size("seq")


def general(tokens, cotangent, gate_weight, first_factor, middle_factor, last_factor):
    width = tokens.shape[-1]
    rows = tokens.reshape(-1, width)
    gate = jax.nn.sigmoid(jnp.dot(rows, gate_weight, preferred_element_type=F32))
    gate = gate.reshape(tokens.shape)
    first_out = mixing(first_factor, tokens, "hab,bjkhe->ajkhe").astype(BF16)
    last_in = send_last(first_out)
    last_out = mixing(last_factor, last_in, "hab,ijbhe->ijahe").astype(BF16)
    middle_in = send_middle(last_out)
    middle_out = mixing(middle_factor, middle_in, "hab,ibkhe->iakhe").astype(BF16)
    mixer = return_last(return_middle(middle_out))
    upstream = cotangent.astype(F32)
    d_mix = (upstream * gate).astype(BF16)
    d_pre = (upstream * mixer.astype(F32) * gate * (1.0 - gate)).astype(BF16)
    pre_rows = d_pre.reshape(-1, width)
    gate_part = jnp.einsum("tc,td->cd", rows, pre_rows, preferred_element_type=F32)
    gate_term = jnp.einsum("td,cd->tc", pre_rows, gate_weight, preferred_element_type=F32)
    middle_grad_in = send_middle(send_last(d_mix))
    middle_back = mixing(middle_factor, middle_grad_in, "hba,ibkhe->iakhe").astype(BF16)
    middle_part = contract(middle_grad_in, middle_in, "iakhe,ibkhe->hab")
    last_back_in = return_middle(middle_back)
    last_back = mixing(last_factor, last_back_in, "hba,ijbhe->ijahe").astype(BF16)
    last_part = contract(last_back_in, last_in, "ijahe,ijbhe->hab")
    first_back_in = return_last(last_back)
    first_back = mixing(first_factor, first_back_in, "hba,bjkhe->ajkhe")
    first_part = contract(first_back_in, tokens, "ajkhe,bjkhe->hab")
    d_tokens = (first_back.reshape(-1, width) + gate_term).astype(BF16).reshape(tokens.shape)
    return (d_tokens,) + reduced(
        gate_part, first_part, middle_part, last_part, 1.0 / math.sqrt(positions(tokens))
    )


def reduced(gate_part, first_part, middle_part, last_part, factor):
    gate_share = lax.psum_scatter(gate_part, "seq", scatter_dimension=0, tiled=True)
    last_share = lax.psum_scatter(last_part, "seq", scatter_dimension=1, tiled=True)
    middle_share = lax.psum_scatter(middle_part, "grp", scatter_dimension=1, tiled=True)
    gate_sum, last_sum, first_half = lax.psum((gate_share, last_share, first_part), "grp")
    middle_sum, first_sum = lax.psum((middle_share, first_half), "seq")
    return gate_sum * factor, first_sum * factor, middle_sum * factor, last_sum * factor


def exchange(values):
    return lax.all_to_all(values, ALL, split_axis=0, concat_axis=0, tiled=True)


def dot(left, right):
    return jnp.dot(left, right, preferred_element_type=F32)


def dot_rows(left, right):
    return lax.dot_general(left, right, (((1,), (1,)), ((), ())), preferred_element_type=F32)


def spread(factor, lanes, turned=False):
    size = factor.shape[0]
    wide = size * lanes
    rows = lax.broadcasted_iota(jnp.int32, (wide, size), 0) // lanes
    tall = jnp.where(rows == lax.broadcasted_iota(jnp.int32, (wide, size), 1), 1.0, 0.0).astype(BF16)
    columns = lax.broadcasted_iota(jnp.int32, (size, wide), 1) // lanes
    flat = jnp.where(columns == lax.broadcasted_iota(jnp.int32, (size, wide), 0), 1.0, 0.0).astype(BF16)
    picked = (dot_rows if turned else dot)(tall, factor).astype(BF16)
    row = lax.broadcasted_iota(jnp.int32, (wide, wide), 0) % lanes
    column = lax.broadcasted_iota(jnp.int32, (wide, wide), 1) % lanes
    return jnp.where(row == column, dot(picked, flat), 0.0).astype(BF16)


def gather_diagonal(total, size, lanes):
    wide = size * lanes
    row = lax.broadcasted_iota(jnp.int32, (wide, wide), 0) % lanes
    column = lax.broadcasted_iota(jnp.int32, (wide, wide), 1) % lanes
    kept = jnp.where(row == column, total, 0.0).reshape(size, lanes, wide).sum(axis=1)
    owner = lax.broadcasted_iota(jnp.int32, (wide, size), 0) // lanes
    target = lax.broadcasted_iota(jnp.int32, (wide, size), 1)
    collect = jnp.where(owner == target, 1.0, 0.0)
    return jnp.dot(kept, collect, precision=lax.Precision.HIGHEST, preferred_element_type=F32)


def gate_of(rows, weight):
    return jax.nn.sigmoid(dot(rows, weight))


def open_kernel(n_i, step_j, lanes, width, x_ref, g_ref, w_ref, a_ref, v_ref, wide):
    size = width // HEADS

    @pl.when(pl.program_id(0) == 0)
    def _():
        for h in range(HEADS):
            wide[h] = spread(a_ref[h], lanes, turned=True)

    sent = []
    for j in range(step_j):
        rows = x_ref[:, j].reshape(n_i * lanes, width)
        up = g_ref[:, j].reshape(n_i * lanes, width).astype(F32)
        sent.append((up * gate_of(rows, w_ref[...])).astype(BF16))
    for h in range(HEADS):
        pair = jnp.concatenate([d[:, h * size : (h + 1) * size] for d in sent], axis=1)
        out = dot(wide[h], pair).astype(BF16)
        for j in range(step_j):
            v_ref[:, j, :, h * size : (h + 1) * size] = out[:, j * size : (j + 1) * size].reshape(
                n_i, lanes, size
            )


def open_side(tokens, cotangent, gate_weight, first_factor):
    n_i, n_j, lanes, width = tokens.shape
    step_j = 2
    block = pl.BlockSpec((n_i, step_j, lanes, width), lambda j: (0, j, 0, 0))
    whole = lambda a: pl.BlockSpec(a.shape, lambda j: (0,) * a.ndim)
    count = tokens.size
    return pl.pallas_call(
        functools.partial(open_kernel, n_i, step_j, lanes, width),
        grid=(n_j // step_j,),
        in_specs=[block, block, whole(gate_weight), whole(first_factor)],
        out_specs=block,
        out_shape=jax.ShapeDtypeStruct(tokens.shape, BF16),
        scratch_shapes=[pltpu.VMEM((HEADS, n_i * lanes, n_i * lanes), BF16)],
        cost_estimate=pl.CostEstimate(
            flops=2 * count * (width + n_i * lanes), bytes_accessed=6 * count, transcendentals=count
        ),
        name="open_side",
    )(tokens, cotangent, gate_weight, first_factor)


def forward_kernel(groups, blocks, n_j, lanes, size, x_ref, b_ref, c_ref, bx_ref, y_ref, wide):
    last = b_ref[0]
    wide[...] = spread(c_ref[0], lanes)

    def over_last(t, carry):
        g, j = t // (n_j // 2), (t % (n_j // 2)) * 2
        pair = [x_ref[g, :, j + p].reshape(blocks * lanes, size) for p in range(2)]
        out = dot(last, jnp.concatenate(pair, axis=1)).astype(BF16)
        for p in range(2):
            bx_ref[g, :, j + p] = out[:, p * size : (p + 1) * size].reshape(blocks, lanes, size)
        return carry

    lax.fori_loop(0, groups * n_j // 2, over_last, 0, unroll=2)

    def over_middle(t, carry):
        pair = [bx_ref[:, 2 * t + p].reshape(groups * n_j * lanes, size) for p in range(2)]
        out = dot(wide[...], jnp.concatenate(pair, axis=1)).astype(BF16)
        for p in range(2):
            y_ref[:, 2 * t + p] = out[:, p * size : (p + 1) * size].reshape(groups, n_j, lanes, size)
        return carry

    lax.fori_loop(0, blocks // 2, over_middle, 0)


def forward_side(values, last_factor, middle_factor):
    groups, blocks, n_j, lanes, width = values.shape
    size = width // HEADS
    block = pl.BlockSpec((groups, blocks, n_j, lanes, size), lambda h: (0, 0, 0, 0, h))
    one = lambda a: pl.BlockSpec((1,) + a.shape[1:], lambda h: (h, 0, 0))
    count = values.size
    return pl.pallas_call(
        functools.partial(forward_kernel, groups, blocks, n_j, lanes, size),
        grid=(HEADS,),
        in_specs=[block, one(last_factor), one(middle_factor)],
        out_specs=[block, block],
        out_shape=[jax.ShapeDtypeStruct(values.shape, BF16)] * 2,
        scratch_shapes=[pltpu.VMEM((groups * n_j * lanes, groups * n_j * lanes), BF16)],
        cost_estimate=pl.CostEstimate(
            flops=2 * count * (middle_factor.shape[1] * lanes + last_factor.shape[1]),
            bytes_accessed=6 * count,
            transcendentals=0,
        ),
        name="forward_side",
    )(values, last_factor, middle_factor)


def backward_kernel(
    groups, blocks, n_j, lanes, size, v_ref, x_ref, bx_ref, b_ref, c_ref, u_ref, gl_ref, gm_ref, cv, acc, wide
):
    rows = groups * n_j * lanes
    wide[...] = spread(c_ref[0], lanes, turned=True)
    acc[...] = jnp.zeros_like(acc)

    def over_middle(t, carry):
        pair = [v_ref[:, 2 * t + p].reshape(rows, size) for p in range(2)]
        sent = jnp.concatenate(pair, axis=1)
        held = [bx_ref[:, 2 * t + p].reshape(rows, size) for p in range(2)]
        acc[...] += dot_rows(sent, jnp.concatenate(held, axis=1))
        out = dot(wide[...], sent).astype(BF16)
        for p in range(2):
            cv[:, 2 * t + p] = out[:, p * size : (p + 1) * size].reshape(groups, n_j, lanes, size)
        return carry

    lax.fori_loop(0, blocks // 2, over_middle, 0)
    gm_ref[0] = gather_diagonal(acc[...], groups * n_j, lanes)
    last = b_ref[0]

    def over_last(t, total):
        g, j = t // (n_j // 2), (t % (n_j // 2)) * 2
        pair = [cv[g, :, j + p].reshape(blocks * lanes, size) for p in range(2)]
        back = jnp.concatenate(pair, axis=1)
        held = [x_ref[g, :, j + p].reshape(blocks * lanes, size) for p in range(2)]
        out = dot(last, back).astype(BF16)
        for p in range(2):
            u_ref[g, :, j + p] = out[:, p * size : (p + 1) * size].reshape(blocks, lanes, size)
        return total + dot_rows(back, jnp.concatenate(held, axis=1))

    zero = jnp.zeros((blocks * lanes, blocks * lanes), F32)
    gl_ref[0] = lax.fori_loop(0, groups * n_j // 2, over_last, zero, unroll=2)


def backward_side(sent, values, mixed, last_factor_t, middle_factor):
    groups, blocks, n_j, lanes, width = values.shape
    size = width // HEADS
    n_middle, n_last = groups * n_j, blocks * lanes
    block = pl.BlockSpec((groups, blocks, n_j, lanes, size), lambda h: (0, 0, 0, 0, h))
    one = lambda *shape: pl.BlockSpec((1,) + shape, lambda h: (h, 0, 0))
    count = values.size
    return pl.pallas_call(
        functools.partial(backward_kernel, groups, blocks, n_j, lanes, size),
        grid=(HEADS,),
        in_specs=[block] * 3 + [one(n_last, n_last), one(n_middle, n_middle)],
        out_specs=[block, one(n_last, n_last), one(n_middle, n_middle)],
        out_shape=[
            jax.ShapeDtypeStruct(values.shape, BF16),
            jax.ShapeDtypeStruct((HEADS, n_last, n_last), F32),
            jax.ShapeDtypeStruct((HEADS, n_middle, n_middle), F32),
        ],
        scratch_shapes=[
            pltpu.VMEM((groups, blocks, n_j, lanes, size), BF16),
            pltpu.VMEM((n_middle * lanes, n_middle * lanes), F32),
            pltpu.VMEM((n_middle * lanes, n_middle * lanes), BF16),
        ],
        cost_estimate=pl.CostEstimate(
            flops=4 * count * (n_middle * lanes + n_last), bytes_accessed=8 * count, transcendentals=0
        ),
        name="backward_side",
    )(sent, values, mixed, last_factor_t, middle_factor)


def close_kernel(
    n_i, step_j, lanes, width, x_ref, g_ref, y_ref, w_ref, a_ref, t_ref, gg_ref, gf_ref, acc, wide
):
    size = width // HEADS
    rows_n = n_i * lanes

    @pl.when(pl.program_id(0) == 0)
    def _():
        acc[...] = jnp.zeros_like(acc)
        gg_ref[...] = jnp.zeros_like(gg_ref)
        for h in range(HEADS):
            wide[h] = spread(a_ref[h], lanes)

    rows, ups, gates, mixes, sent = [], [], [], [], []
    for j in range(step_j):
        rows.append(x_ref[:, j].reshape(rows_n, width))
        ups.append(g_ref[:, j].reshape(rows_n, width).astype(F32))
        gates.append(gate_of(rows[j], w_ref[...]))
        mixes.append(y_ref[:, j].reshape(rows_n, width))
        sent.append((ups[j] * gates[j]).astype(BF16))
    outs = []
    for h in range(HEADS):
        cut = slice(h * size, (h + 1) * size)
        held = jnp.concatenate([m[:, cut] for m in mixes], axis=1)
        back = jnp.concatenate([d[:, cut] for d in sent], axis=1)
        acc[h] += dot_rows(back, held)
        outs.append(dot(wide[h], held).astype(BF16).astype(F32))
    for j in range(step_j):
        mixer = jnp.concatenate([o[:, j * size : (j + 1) * size] for o in outs], axis=1)
        d_pre = (ups[j] * mixer * gates[j] * (1.0 - gates[j])).astype(BF16)
        t_ref[:, j] = dot_rows(d_pre, w_ref[...]).astype(BF16).reshape(n_i, lanes, width)
        gg_ref[...] += lax.dot_general(
            rows[j], d_pre, (((0,), (0,)), ((), ())), preferred_element_type=F32
        )

    @pl.when(pl.program_id(0) == pl.num_programs(0) - 1)
    def _():
        for h in range(HEADS):
            gf_ref[h] = gather_diagonal(acc[h], n_i, lanes)


def close_side(tokens, cotangent, mixed, gate_weight, first_factor):
    n_i, n_j, lanes, width = tokens.shape
    step_j = 2
    block = pl.BlockSpec((n_i, step_j, lanes, width), lambda j: (0, j, 0, 0))
    whole = lambda shape: pl.BlockSpec(shape, lambda j: (0,) * len(shape))
    count = tokens.size
    return pl.pallas_call(
        functools.partial(close_kernel, n_i, step_j, lanes, width),
        grid=(n_j // step_j,),
        in_specs=[block, block, block, whole(gate_weight.shape), whole(first_factor.shape)],
        out_specs=[block, whole((width, width)), whole((HEADS, n_i, n_i))],
        out_shape=[
            jax.ShapeDtypeStruct(tokens.shape, BF16),
            jax.ShapeDtypeStruct((width, width), F32),
            jax.ShapeDtypeStruct((HEADS, n_i, n_i), F32),
        ],
        scratch_shapes=[
            pltpu.VMEM((HEADS, n_i * lanes, n_i * lanes), F32),
            pltpu.VMEM((HEADS, n_i * lanes, n_i * lanes), BF16),
        ],
        cost_estimate=pl.CostEstimate(
            flops=2 * count * (3 * width + 2 * n_i * lanes),
            bytes_accessed=8 * count,
            transcendentals=count,
        ),
        name="close_side",
    )(tokens, cotangent, mixed, gate_weight, first_factor)


def direct(tokens, cotangent, gate_weight, first_factor, middle_factor, last_factor):
    groups, blocks = lax.axis_size("grp"), lax.axis_size("seq")
    split = (groups, blocks) + tokens.shape[1:]
    at_whole = exchange(tokens).reshape(split)
    sent = open_side(tokens, cotangent, gate_weight, first_factor)
    sent_whole = exchange(sent).reshape(split)
    mixed, forward = forward_side(at_whole, last_factor, middle_factor)
    forward_home = exchange(forward.reshape(tokens.shape))
    backward, last_part, middle_part = backward_side(
        sent_whole, at_whole, mixed, last_factor.transpose(0, 2, 1), middle_factor
    )
    back_home = exchange(backward.reshape(tokens.shape))
    gate_term, gate_part, first_part = close_side(
        tokens, cotangent, forward_home, gate_weight, first_factor
    )
    d_tokens = (back_home.astype(F32) + gate_term.astype(F32)).astype(BF16)
    return (d_tokens,) + reduced(
        gate_part, first_part, middle_part, last_part, 1.0 / math.sqrt(positions(tokens))
    )


def shards(tokens, *others):
    n_i, n_j, lanes, width = tokens.shape
    groups, blocks = lax.axis_size("grp"), lax.axis_size("seq")
    whole_tiles = lanes % 16 == 0 and n_j % 2 == 0 and blocks % 2 == 0
    if n_i == groups * blocks and whole_tiles and width % (HEADS * 128) == 0:
        return direct(tokens, *others)
    return general(tokens, *others)


def solution(mesh):
    in_specs = (P(None, "grp", "seq", None), P(None, "grp", "seq", None), P(), P(), P(), P())
    out_specs = (
        P(None, "grp", "seq", None),
        P("seq", None),
        P(),
        P(None, "grp", None),
        P(None, "seq", None),
    )
    return jax.shard_map(shards, mesh=mesh, in_specs=in_specs, out_specs=out_specs, check_vma=False)
```

```python
import functools
import math

import jax
import jax.numpy as jnp
from jax import lax
from jax.experimental import pallas as pl
from jax.experimental.pallas import tpu as pltpu
from jax.sharding import PartitionSpec as P


HEADS = 4
EARLY = 3
ALL = ("grp", "seq")
F32 = jnp.float32
BF16 = jnp.bfloat16


def headed(values):
    return values.reshape(values.shape[:-1] + (HEADS, values.shape[-1] // HEADS))


def mixing(weights, values, form):
    result = jnp.einsum(form, weights, headed(values), preferred_element_type=F32)
    return result.reshape(values.shape)


def contract(left, right, form):
    return jnp.einsum(form, headed(left), headed(right), preferred_element_type=F32)


def send_last(values):
    return lax.all_to_all(values, "seq", split_axis=0, concat_axis=2, tiled=True)


def send_middle(values):
    return lax.all_to_all(values, "grp", split_axis=2, concat_axis=1, tiled=True)


def return_middle(values):
    return lax.all_to_all(values, "grp", split_axis=1, concat_axis=2, tiled=True)


def return_last(values):
    return lax.all_to_all(values, "seq", split_axis=2, concat_axis=0, tiled=True)


def positions(tokens):
    return math.prod(tokens.shape[:3]) * lax.axis_size("grp") * lax.axis_size("seq")


def general(tokens, cotangent, gate_weight, first_factor, middle_factor, last_factor):
    width = tokens.shape[-1]
    rows = tokens.reshape(-1, width)
    gate = jax.nn.sigmoid(jnp.dot(rows, gate_weight, preferred_element_type=F32))
    gate = gate.reshape(tokens.shape)
    first_out = mixing(first_factor, tokens, "hab,bjkhe->ajkhe").astype(BF16)
    last_in = send_last(first_out)
    last_out = mixing(last_factor, last_in, "hab,ijbhe->ijahe").astype(BF16)
    middle_in = send_middle(last_out)
    middle_out = mixing(middle_factor, middle_in, "hab,ibkhe->iakhe").astype(BF16)
    mixer = return_last(return_middle(middle_out))
    upstream = cotangent.astype(F32)
    d_mix = (upstream * gate).astype(BF16)
    d_pre = (upstream * mixer.astype(F32) * gate * (1.0 - gate)).astype(BF16)
    pre_rows = d_pre.reshape(-1, width)
    gate_part = jnp.einsum("tc,td->cd", rows, pre_rows, preferred_element_type=F32)
    gate_term = jnp.einsum("td,cd->tc", pre_rows, gate_weight, preferred_element_type=F32)
    middle_grad_in = send_middle(send_last(d_mix))
    middle_back = mixing(middle_factor, middle_grad_in, "hba,ibkhe->iakhe").astype(BF16)
    middle_part = contract(middle_grad_in, middle_in, "iakhe,ibkhe->hab")
    last_back_in = return_middle(middle_back)
    last_back = mixing(last_factor, last_back_in, "hba,ijbhe->ijahe").astype(BF16)
    last_part = contract(last_back_in, last_in, "ijahe,ijbhe->hab")
    first_back_in = return_last(last_back)
    first_back = mixing(first_factor, first_back_in, "hba,bjkhe->ajkhe")
    first_part = contract(first_back_in, tokens, "ajkhe,bjkhe->hab")
    d_tokens = (first_back.reshape(-1, width) + gate_term).astype(BF16).reshape(tokens.shape)
    return (d_tokens,) + reduced(
        gate_part, first_part, middle_part, last_part, 1.0 / math.sqrt(positions(tokens))
    )


def reduced(gate_part, first_part, middle_part, last_part, factor):
    gate_share = lax.psum_scatter(gate_part, "seq", scatter_dimension=0, tiled=True)
    last_share = lax.psum_scatter(last_part, "seq", scatter_dimension=1, tiled=True)
    middle_share = lax.psum_scatter(middle_part, "grp", scatter_dimension=1, tiled=True)
    gate_sum, last_sum, first_half = lax.psum((gate_share, last_share, first_part), "grp")
    middle_sum, first_sum = lax.psum((middle_share, first_half), "seq")
    return gate_sum * factor, first_sum * factor, middle_sum * factor, last_sum * factor


def exchange(values):
    return lax.all_to_all(values, ALL, split_axis=0, concat_axis=0, tiled=True)


def dot(left, right):
    return jnp.dot(left, right, preferred_element_type=F32)


def dot_rows(left, right):
    return lax.dot_general(left, right, (((1,), (1,)), ((), ())), preferred_element_type=F32)


def spread(factor, lanes, turned=False):
    size = factor.shape[0]
    wide = size * lanes
    rows = lax.broadcasted_iota(jnp.int32, (wide, size), 0) // lanes
    tall = jnp.where(rows == lax.broadcasted_iota(jnp.int32, (wide, size), 1), 1.0, 0.0).astype(BF16)
    columns = lax.broadcasted_iota(jnp.int32, (size, wide), 1) // lanes
    flat = jnp.where(columns == lax.broadcasted_iota(jnp.int32, (size, wide), 0), 1.0, 0.0).astype(BF16)
    picked = (dot_rows if turned else dot)(tall, factor).astype(BF16)
    row = lax.broadcasted_iota(jnp.int32, (wide, wide), 0) % lanes
    column = lax.broadcasted_iota(jnp.int32, (wide, wide), 1) % lanes
    return jnp.where(row == column, dot(picked, flat), 0.0).astype(BF16)


def gather_diagonal(total, size, lanes):
    wide = size * lanes
    row = lax.broadcasted_iota(jnp.int32, (wide, wide), 0) % lanes
    column = lax.broadcasted_iota(jnp.int32, (wide, wide), 1) % lanes
    kept = jnp.where(row == column, total, 0.0).reshape(size, lanes, wide).sum(axis=1)
    owner = lax.broadcasted_iota(jnp.int32, (wide, size), 0) // lanes
    target = lax.broadcasted_iota(jnp.int32, (wide, size), 1)
    collect = jnp.where(owner == target, 1.0, 0.0)
    return jnp.dot(kept, collect, precision=lax.Precision.HIGHEST, preferred_element_type=F32)


def gate_of(rows, weight):
    return jax.nn.sigmoid(dot(rows, weight))


def open_kernel(n_i, step_j, lanes, width, x_ref, g_ref, w_ref, a_ref, v_ref, wide):
    size = width // HEADS

    @pl.when(pl.program_id(0) == 0)
    def _():
        for h in range(HEADS):
            wide[h] = spread(a_ref[h], lanes, turned=True)

    sent = []
    for j in range(step_j):
        rows = x_ref[:, j].reshape(n_i * lanes, width)
        up = g_ref[:, j].reshape(n_i * lanes, width).astype(F32)
        sent.append((up * gate_of(rows, w_ref[...])).astype(BF16))
    for h in range(HEADS):
        pair = jnp.concatenate([d[:, h * size : (h + 1) * size] for d in sent], axis=1)
        out = dot(wide[h], pair).astype(BF16)
        for j in range(step_j):
            v_ref[:, j, :, h * size : (h + 1) * size] = out[:, j * size : (j + 1) * size].reshape(
                n_i, lanes, size
            )


def open_side(tokens, cotangent, gate_weight, first_factor):
    n_i, n_j, lanes, width = tokens.shape
    step_j = 2
    block = pl.BlockSpec((n_i, step_j, lanes, width), lambda j: (0, j, 0, 0))
    whole = lambda a: pl.BlockSpec(a.shape, lambda j: (0,) * a.ndim)
    count = tokens.size
    return pl.pallas_call(
        functools.partial(open_kernel, n_i, step_j, lanes, width),
        grid=(n_j // step_j,),
        in_specs=[block, block, whole(gate_weight), whole(first_factor)],
        out_specs=block,
        out_shape=jax.ShapeDtypeStruct(tokens.shape, BF16),
        scratch_shapes=[pltpu.VMEM((HEADS, n_i * lanes, n_i * lanes), BF16)],
        cost_estimate=pl.CostEstimate(
            flops=2 * count * (width + n_i * lanes), bytes_accessed=6 * count, transcendentals=count
        ),
        name="open_side",
    )(tokens, cotangent, gate_weight, first_factor)


def forward_kernel(groups, blocks, n_j, lanes, size, x_ref, b_ref, c_ref, bx_ref, y_ref, wide):
    last = b_ref[0]
    wide[...] = spread(c_ref[0], lanes)

    def over_last(t, carry):
        g, j = t // (n_j // 2), (t % (n_j // 2)) * 2
        pair = [x_ref[g, :, j + p].reshape(blocks * lanes, size) for p in range(2)]
        out = dot(last, jnp.concatenate(pair, axis=1)).astype(BF16)
        for p in range(2):
            bx_ref[g, :, j + p] = out[:, p * size : (p + 1) * size].reshape(blocks, lanes, size)
        return carry

    lax.fori_loop(0, groups * n_j // 2, over_last, 0, unroll=2)

    def over_middle(t, carry):
        pair = [bx_ref[:, 2 * t + p].reshape(groups * n_j * lanes, size) for p in range(2)]
        out = dot(wide[...], jnp.concatenate(pair, axis=1)).astype(BF16)
        for p in range(2):
            y_ref[:, 2 * t + p] = out[:, p * size : (p + 1) * size].reshape(groups, n_j, lanes, size)
        return carry

    lax.fori_loop(0, blocks // 2, over_middle, 0)


def forward_side(values, last_factor, middle_factor):
    groups, blocks, n_j, lanes, width = values.shape
    size = width // HEADS
    block = pl.BlockSpec((groups, blocks, n_j, lanes, size), lambda h: (0, 0, 0, 0, h))
    one = lambda a: pl.BlockSpec((1,) + a.shape[1:], lambda h: (h, 0, 0))
    count = values.size
    return pl.pallas_call(
        functools.partial(forward_kernel, groups, blocks, n_j, lanes, size),
        grid=(HEADS,),
        in_specs=[block, one(last_factor), one(middle_factor)],
        out_specs=[block, block],
        out_shape=[jax.ShapeDtypeStruct(values.shape, BF16)] * 2,
        scratch_shapes=[pltpu.VMEM((groups * n_j * lanes, groups * n_j * lanes), BF16)],
        cost_estimate=pl.CostEstimate(
            flops=2 * count * (middle_factor.shape[1] * lanes + last_factor.shape[1]),
            bytes_accessed=6 * count,
            transcendentals=0,
        ),
        name="forward_side",
    )(values, last_factor, middle_factor)


def backward_kernel(
    groups, blocks, n_j, lanes, size, v_ref, x_ref, bx_ref, b_ref, c_ref, early_ref, late_ref, gl_ref,
    gm_ref, cv, acc, wide
):
    rows = groups * n_j * lanes
    is_early = pl.program_id(0) < EARLY
    wide[...] = spread(c_ref[0], lanes, turned=True)
    acc[...] = jnp.zeros_like(acc)

    def over_middle(t, carry):
        pair = [v_ref[:, 2 * t + p].reshape(rows, size) for p in range(2)]
        sent = jnp.concatenate(pair, axis=1)
        held = [bx_ref[:, 2 * t + p].reshape(rows, size) for p in range(2)]
        acc[...] += dot_rows(sent, jnp.concatenate(held, axis=1))
        out = dot(wide[...], sent).astype(BF16)
        for p in range(2):
            cv[:, 2 * t + p] = out[:, p * size : (p + 1) * size].reshape(groups, n_j, lanes, size)
        return carry

    lax.fori_loop(0, blocks // 2, over_middle, 0)
    gm_ref[0] = gather_diagonal(acc[...], groups * n_j, lanes)
    last = b_ref[0]

    def over_last(t, total):
        g, j = t // (n_j // 2), (t % (n_j // 2)) * 2
        pair = [cv[g, :, j + p].reshape(blocks * lanes, size) for p in range(2)]
        back = jnp.concatenate(pair, axis=1)
        held = [x_ref[g, :, j + p].reshape(blocks * lanes, size) for p in range(2)]
        out = dot(last, back).astype(BF16)
        for p in range(2):
            piece = out[:, p * size : (p + 1) * size].reshape(blocks, lanes, size)

            @pl.when(is_early)
            def _():
                early_ref[g, :, j + p] = piece

            @pl.when(jnp.logical_not(is_early))
            def _():
                late_ref[g, :, j + p] = piece

        return total + dot_rows(back, jnp.concatenate(held, axis=1))

    zero = jnp.zeros((blocks * lanes, blocks * lanes), F32)
    gl_ref[0] = lax.fori_loop(0, groups * n_j // 2, over_last, zero, unroll=2)


def backward_side(sent, values, mixed, last_factor_t, middle_factor):
    groups, blocks, n_j, lanes, width = values.shape
    size = width // HEADS
    n_middle, n_last = groups * n_j, blocks * lanes
    block = pl.BlockSpec((groups, blocks, n_j, lanes, size), lambda h: (0, 0, 0, 0, h))
    one = lambda *shape: pl.BlockSpec((1,) + shape, lambda h: (h, 0, 0))
    count = values.size
    return pl.pallas_call(
        functools.partial(backward_kernel, groups, blocks, n_j, lanes, size),
        grid=(HEADS,),
        in_specs=[block] * 3 + [one(n_last, n_last), one(n_middle, n_middle)],
        out_specs=[
            pl.BlockSpec(block.block_shape, lambda h: (0, 0, 0, 0, jnp.minimum(h, EARLY - 1))),
            pl.BlockSpec(block.block_shape, lambda h: (0, 0, 0, 0, jnp.maximum(h - EARLY, 0))),
            one(n_last, n_last),
            one(n_middle, n_middle),
        ],
        out_shape=[
            jax.ShapeDtypeStruct(values.shape[:-1] + (EARLY * size,), BF16),
            jax.ShapeDtypeStruct(values.shape[:-1] + (width - EARLY * size,), BF16),
            jax.ShapeDtypeStruct((HEADS, n_last, n_last), F32),
            jax.ShapeDtypeStruct((HEADS, n_middle, n_middle), F32),
        ],
        scratch_shapes=[
            pltpu.VMEM((groups, blocks, n_j, lanes, size), BF16),
            pltpu.VMEM((n_middle * lanes, n_middle * lanes), F32),
            pltpu.VMEM((n_middle * lanes, n_middle * lanes), BF16),
        ],
        cost_estimate=pl.CostEstimate(
            flops=4 * count * (n_middle * lanes + n_last), bytes_accessed=8 * count, transcendentals=0
        ),
        name="backward_side",
    )(sent, values, mixed, last_factor_t, middle_factor)


def close_kernel(
    n_i, step_j, lanes, width, x_ref, g_ref, y_ref, w_ref, a_ref, t_ref, gg_ref, gf_ref, acc, wide
):
    size = width // HEADS
    rows_n = n_i * lanes

    @pl.when(pl.program_id(0) == 0)
    def _():
        acc[...] = jnp.zeros_like(acc)
        gg_ref[...] = jnp.zeros_like(gg_ref)
        for h in range(HEADS):
            wide[h] = spread(a_ref[h], lanes)

    rows, ups, gates, mixes, sent = [], [], [], [], []
    for j in range(step_j):
        rows.append(x_ref[:, j].reshape(rows_n, width))
        ups.append(g_ref[:, j].reshape(rows_n, width).astype(F32))
        gates.append(gate_of(rows[j], w_ref[...]))
        mixes.append(y_ref[:, j].reshape(rows_n, width))
        sent.append((ups[j] * gates[j]).astype(BF16))
    outs = []
    for h in range(HEADS):
        cut = slice(h * size, (h + 1) * size)
        held = jnp.concatenate([m[:, cut] for m in mixes], axis=1)
        back = jnp.concatenate([d[:, cut] for d in sent], axis=1)
        acc[h] += dot_rows(back, held)
        outs.append(dot(wide[h], held).astype(BF16).astype(F32))
    for j in range(step_j):
        mixer = jnp.concatenate([o[:, j * size : (j + 1) * size] for o in outs], axis=1)
        d_pre = (ups[j] * mixer * gates[j] * (1.0 - gates[j])).astype(BF16)
        t_ref[:, j] = dot_rows(d_pre, w_ref[...]).astype(BF16).reshape(n_i, lanes, width)
        gg_ref[...] += lax.dot_general(
            rows[j], d_pre, (((0,), (0,)), ((), ())), preferred_element_type=F32
        )

    @pl.when(pl.program_id(0) == pl.num_programs(0) - 1)
    def _():
        for h in range(HEADS):
            gf_ref[h] = gather_diagonal(acc[h], n_i, lanes)


def close_side(tokens, cotangent, mixed, gate_weight, first_factor):
    n_i, n_j, lanes, width = tokens.shape
    step_j = 2
    block = pl.BlockSpec((n_i, step_j, lanes, width), lambda j: (0, j, 0, 0))
    whole = lambda shape: pl.BlockSpec(shape, lambda j: (0,) * len(shape))
    count = tokens.size
    return pl.pallas_call(
        functools.partial(close_kernel, n_i, step_j, lanes, width),
        grid=(n_j // step_j,),
        in_specs=[block, block, block, whole(gate_weight.shape), whole(first_factor.shape)],
        out_specs=[block, whole((width, width)), whole((HEADS, n_i, n_i))],
        out_shape=[
            jax.ShapeDtypeStruct(tokens.shape, BF16),
            jax.ShapeDtypeStruct((width, width), F32),
            jax.ShapeDtypeStruct((HEADS, n_i, n_i), F32),
        ],
        scratch_shapes=[
            pltpu.VMEM((HEADS, n_i * lanes, n_i * lanes), F32),
            pltpu.VMEM((HEADS, n_i * lanes, n_i * lanes), BF16),
        ],
        cost_estimate=pl.CostEstimate(
            flops=2 * count * (3 * width + 2 * n_i * lanes),
            bytes_accessed=8 * count,
            transcendentals=count,
        ),
        name="close_side",
    )(tokens, cotangent, mixed, gate_weight, first_factor)


def finish_kernel(b_ref, t_ref, *refs):
    refs[-1][...] = (b_ref[...].astype(F32) + t_ref[...].astype(F32)).astype(BF16)


def finish(back, gate_term, offset, held=None):
    n_i, n_j, lanes, width = gate_term.shape
    size = width // HEADS
    step = n_i // 4
    here = pl.BlockSpec((step, n_j, lanes, size), lambda h, i: (i, 0, 0, h))
    there = pl.BlockSpec((step, n_j, lanes, size), lambda h, i: (i, 0, 0, h + offset))
    more = [] if held is None else [held]
    return pl.pallas_call(
        finish_kernel,
        grid=(back.shape[-1] // size, n_i // step),
        in_specs=[here, there] + [pl.BlockSpec(memory_space=pl.ANY)] * len(more),
        out_specs=there,
        out_shape=jax.ShapeDtypeStruct(gate_term.shape, BF16),
        input_output_aliases={2: 0} if more else {},
        cost_estimate=pl.CostEstimate(flops=back.size, bytes_accessed=6 * back.size, transcendentals=0),
    )(back, gate_term, *more)


def shifted(parts, axis):
    count = lax.axis_size(axis)
    me = lax.axis_index(axis)
    out = []
    for d in range(1, count):
        part = lax.dynamic_index_in_dim(parts, (me + d) % count, 0, False)
        out.append(lax.ppermute(part, axis, [(i, (i + d) % count) for i in range(count)]))
    return out


def share_kernel(factor, *refs):
    total = refs[0][...]
    for part in refs[1:-1]:
        total += part[...]
    refs[-1][...] = total * factor


def share_sum(parts, factor):
    return pl.pallas_call(
        functools.partial(share_kernel, factor),
        out_shape=jax.ShapeDtypeStruct(parts[0].shape, F32),
        name="share_sum",
    )(*parts)


def ordered_kernel(axis, *refs):
    parts, out_ref, held = refs[:-2], refs[-2], refs[-1]
    count = len(parts)
    me = lax.axis_index(axis)
    for d, part in enumerate(parts):
        held[d] = part[...]
    total = held[lax.rem(me + count, count)]
    for source in range(1, count):
        total += held[lax.rem(me - source + count, count)]
    out_ref[...] = total


def ordered_sum(parts, axis):
    shape = parts[0].shape
    return pl.pallas_call(
        functools.partial(ordered_kernel, axis),
        out_shape=jax.ShapeDtypeStruct(shape, F32),
        scratch_shapes=[pltpu.VMEM((len(parts),) + shape, F32)],
        name="ordered_sum",
    )(*parts)


def reduced_direct(gate_part, first_part, middle_part, last_part, factor):
    groups, blocks = lax.axis_size("grp"), lax.axis_size("seq")
    width = gate_part.shape[0]
    n_last, n_middle, n_first = last_part.shape[1], middle_part.shape[1], first_part.shape[1]
    lane = width // groups
    own = HEADS // groups

    def flat(parts):
        return parts.reshape(parts.shape[0], -1, lane)

    packed = jnp.concatenate(
        [
            gate_part.reshape(width, groups, lane).transpose(1, 0, 2),
            flat(last_part.reshape(groups, -1)),
            flat(middle_part.reshape(HEADS, groups, -1).transpose(1, 0, 2)),
            flat(first_part.reshape(groups, -1)),
        ],
        axis=1,
    )
    mine = lax.dynamic_index_in_dim(packed, lax.axis_index("grp"), 0, False)
    share = share_sum([mine] + shifted(packed, "grp"), factor)
    cuts = [width, own * n_last * n_last // lane, HEADS * n_middle * n_middle // groups // lane]
    gate, last, middle, first = jnp.split(share, [sum(cuts[: n + 1]) for n in range(3)])
    last = last.reshape(own, blocks, n_last // blocks, n_last).transpose(1, 0, 2, 3)
    again = jnp.concatenate(
        [
            gate.reshape(blocks, -1, lane),
            flat(last.reshape(blocks, -1)),
            jnp.broadcast_to(middle, (blocks,) + middle.shape),
            jnp.broadcast_to(first, (blocks,) + first.shape),
        ],
        axis=1,
    )
    mine = lax.dynamic_index_in_dim(again, lax.axis_index("seq"), 0, False)
    total = ordered_sum([mine] + shifted(again, "seq"), "seq")
    cuts = [width // blocks, own * n_last * n_last // blocks // lane, middle.shape[0]]
    gate, last, middle, first = jnp.split(total, [sum(cuts[: n + 1]) for n in range(3)])
    give = jnp.concatenate([gate, last, first])
    me = lax.axis_index("grp")
    spread_out = jnp.zeros((groups,) + give.shape, F32)
    spread_out = lax.dynamic_update_index_in_dim(spread_out, give, me, 0)
    for d, part in enumerate(shifted(jnp.broadcast_to(give, (groups,) + give.shape), "grp"), 1):
        spread_out = lax.dynamic_update_index_in_dim(spread_out, part, (me - d) % groups, 0)
    gate, last, first = jnp.split(spread_out, [gate.shape[0], gate.shape[0] + last.shape[0]], axis=1)
    return (
        gate.transpose(1, 0, 2).reshape(-1, width),
        first.reshape(HEADS, n_first, n_first),
        middle.reshape(HEADS, n_middle // groups, n_middle),
        last.reshape(HEADS, n_last // blocks, n_last),
    )


def ordered(tokens, cotangent, gate_weight, first_factor, middle_factor, last_factor):
    groups, blocks = lax.axis_size("grp"), lax.axis_size("seq")
    split = (groups, blocks) + tokens.shape[1:]
    at_whole = exchange(tokens).reshape(split)
    sent = open_side(tokens, cotangent, gate_weight, first_factor)
    sent_whole = exchange(sent).reshape(split)
    mixed, forward = forward_side(at_whole, last_factor, middle_factor)
    forward_home = exchange(forward.reshape(tokens.shape))
    early, late, last_part, middle_part = backward_side(
        sent_whole, at_whole, mixed, last_factor.transpose(0, 2, 1), middle_factor
    )
    early_home = exchange(early.reshape(tokens.shape[:-1] + early.shape[-1:]))
    gate_term, gate_part, first_part = close_side(
        tokens, cotangent, forward_home, gate_weight, first_factor
    )
    sums = reduced_direct(
        gate_part, first_part, middle_part, last_part, 1.0 / math.sqrt(positions(tokens))
    )
    late_home = exchange(late.reshape(tokens.shape[:-1] + late.shape[-1:]))
    d_tokens = finish(early_home, gate_term, 0)
    return (finish(late_home, gate_term, EARLY, d_tokens),) + sums


def shards(tokens, *others):
    n_i, n_j, lanes, width = tokens.shape
    groups, blocks = lax.axis_size("grp"), lax.axis_size("seq")
    whole_tiles = lanes % 16 == 0 and n_j % 2 == 0 and blocks % 2 == 0
    lane_sized = width == groups * 128 and HEADS % groups == 0
    if n_i == groups * blocks and whole_tiles and lane_sized and n_i % 4 == 0 and width % (HEADS * 128) == 0:
        return ordered(tokens, *others)
    return general(tokens, *others)


def solution(mesh):
    in_specs = (P(None, "grp", "seq", None), P(None, "grp", "seq", None), P(), P(), P(), P())
    out_specs = (
        P(None, "grp", "seq", None),
        P("seq", None),
        P(),
        P(None, "grp", None),
        P(None, "seq", None),
    )
    return jax.shard_map(shards, mesh=mesh, in_specs=in_specs, out_specs=out_specs, check_vma=False)
```

```python
import functools
import math

import jax
import jax.numpy as jnp
from jax import lax
from jax.experimental import pallas as pl
from jax.experimental.pallas import tpu as pltpu
from jax.sharding import PartitionSpec as P


HEADS = 4
F32 = jnp.float32
BF16 = jnp.bfloat16


def headed(values):
    return values.reshape(values.shape[:-1] + (HEADS, values.shape[-1] // HEADS))


def mixing(weights, values, form):
    result = jnp.einsum(form, weights, headed(values), preferred_element_type=F32)
    return result.reshape(values.shape)


def contract(left, right, form):
    return jnp.einsum(form, headed(left), headed(right), preferred_element_type=F32)


def send_last(values):
    return lax.all_to_all(values, "seq", split_axis=0, concat_axis=2, tiled=True)


def send_middle(values):
    return lax.all_to_all(values, "grp", split_axis=2, concat_axis=1, tiled=True)


def return_middle(values):
    return lax.all_to_all(values, "grp", split_axis=1, concat_axis=2, tiled=True)


def return_last(values):
    return lax.all_to_all(values, "seq", split_axis=2, concat_axis=0, tiled=True)


def positions(tokens, seq):
    return math.prod(tokens.shape[:3]) * lax.axis_size("grp") * lax.axis_size(seq)


def general(tokens, cotangent, gate_weight, first_factor, middle_factor, last_factor):
    width = tokens.shape[-1]
    rows = tokens.reshape(-1, width)
    gate = jax.nn.sigmoid(jnp.dot(rows, gate_weight, preferred_element_type=F32))
    gate = gate.reshape(tokens.shape)
    first_out = mixing(first_factor, tokens, "hab,bjkhe->ajkhe").astype(BF16)
    last_in = send_last(first_out)
    last_out = mixing(last_factor, last_in, "hab,ijbhe->ijahe").astype(BF16)
    middle_in = send_middle(last_out)
    middle_out = mixing(middle_factor, middle_in, "hab,ibkhe->iakhe").astype(BF16)
    mixer = return_last(return_middle(middle_out))
    upstream = cotangent.astype(F32)
    d_mix = (upstream * gate).astype(BF16)
    d_pre = (upstream * mixer.astype(F32) * gate * (1.0 - gate)).astype(BF16)
    pre_rows = d_pre.reshape(-1, width)
    gate_part = jnp.einsum("tc,td->cd", rows, pre_rows, preferred_element_type=F32)
    gate_term = jnp.einsum("td,cd->tc", pre_rows, gate_weight, preferred_element_type=F32)
    middle_grad_in = send_middle(send_last(d_mix))
    middle_back = mixing(middle_factor, middle_grad_in, "hba,ibkhe->iakhe").astype(BF16)
    middle_part = contract(middle_grad_in, middle_in, "iakhe,ibkhe->hab")
    last_back_in = return_middle(middle_back)
    last_back = mixing(last_factor, last_back_in, "hba,ijbhe->ijahe").astype(BF16)
    last_part = contract(last_back_in, last_in, "ijahe,ijbhe->hab")
    first_back_in = return_last(last_back)
    first_back = mixing(first_factor, first_back_in, "hba,bjkhe->ajkhe")
    first_part = contract(first_back_in, tokens, "ajkhe,bjkhe->hab")
    d_tokens = (first_back.reshape(-1, width) + gate_term).astype(BF16).reshape(tokens.shape)
    return (d_tokens,) + reduced(
        gate_part, first_part, middle_part, last_part, 1.0 / math.sqrt(positions(tokens, "seq"))
    )


def reduced(gate_part, first_part, middle_part, last_part, factor):
    gate_share = lax.psum_scatter(gate_part, "seq", scatter_dimension=0, tiled=True)
    last_share = lax.psum_scatter(last_part, "seq", scatter_dimension=1, tiled=True)
    middle_share = lax.psum_scatter(middle_part, "grp", scatter_dimension=1, tiled=True)
    gate_sum, last_sum, first_half = lax.psum((gate_share, last_share, first_part), "grp")
    middle_sum, first_sum = lax.psum((middle_share, first_half), "seq")
    return gate_sum * factor, first_sum * factor, middle_sum * factor, last_sum * factor


PLANES = ("z", "y")


def dot(left, right):
    return jnp.dot(left, right, preferred_element_type=F32)


def dot_rows(left, right):
    return lax.dot_general(left, right, (((1,), (1,)), ((), ())), preferred_element_type=F32)


def exact(left, right):
    return jnp.dot(left, right, precision=lax.Precision.HIGHEST, preferred_element_type=F32)


def iota(shape, axis):
    return lax.broadcasted_iota(jnp.int32, shape, axis)


def place(size, block):
    source = ((iota((size, size), 0) // block) ^ lax.axis_index("z")) * block + iota((size, size), 0) % block
    return jnp.where(source == iota((size, size), 1), 1.0, 0.0)


def spread(factor, lanes, turned=False):
    size = factor.shape[0]
    wide = size * lanes
    tall = jnp.where(iota((wide, size), 0) // lanes == iota((wide, size), 1), 1.0, 0.0).astype(BF16)
    flat = jnp.where(iota((size, wide), 1) // lanes == iota((size, wide), 0), 1.0, 0.0).astype(BF16)
    picked = (dot_rows if turned else dot)(tall, factor).astype(BF16)
    same = iota((wide, wide), 0) % lanes == iota((wide, wide), 1) % lanes
    return jnp.where(same, dot(picked, flat), 0.0).astype(BF16)


def gather_diagonal(total, size, lanes):
    wide = size * lanes
    same = iota((wide, wide), 0) % lanes == iota((wide, wide), 1) % lanes
    kept = jnp.where(same, total, 0.0).reshape(size, lanes, wide).sum(axis=1)
    collect = jnp.where(iota((wide, size), 0) // lanes == iota((wide, size), 1), 1.0, 0.0)
    return exact(kept, collect)


def gate_of(rows, weight):
    return jax.nn.sigmoid(dot(rows, weight))


def open_kernel(planes, step_j, x_ref, g_ref, w_ref, a_ref, *refs):
    v_refs, wide = refs[:planes], refs[planes]
    n_i, _, lanes, width = x_ref.shape
    size, part = width // HEADS, n_i // planes

    @pl.when(pl.program_id(0) == 0)
    def _():
        moved = place(n_i, part).astype(BF16)
        for h in range(HEADS):
            wide[h] = spread(dot_rows(a_ref[h], moved).astype(BF16), lanes, turned=True)

    sent = []
    for j in range(step_j):
        rows = x_ref[:, j].reshape(n_i * lanes, width)
        up = g_ref[:, j].reshape(n_i * lanes, width).astype(F32)
        sent.append((up * gate_of(rows, w_ref[...])).astype(BF16))
    for h in range(HEADS):
        pair = jnp.concatenate([d[:, h * size : (h + 1) * size] for d in sent], axis=1)
        out = dot(wide[h], pair).astype(BF16)
        for m in range(planes):
            for j in range(step_j):
                piece = out[m * part * lanes : (m + 1) * part * lanes, j * size : (j + 1) * size]
                v_refs[m][:, j, :, h * size : (h + 1) * size] = piece.reshape(part, lanes, size)


def open_side(tokens, cotangent, gate_weight, first_factor, planes):
    n_i, n_j, lanes, width = tokens.shape
    step_j = 2
    block = pl.BlockSpec((n_i, step_j, lanes, width), lambda j: (0, j, 0, 0))
    part = pl.BlockSpec((n_i // planes, step_j, lanes, width), lambda j: (0, j, 0, 0))
    whole = lambda a: pl.BlockSpec(a.shape, lambda j: (0,) * a.ndim)
    count = tokens.size
    return pl.pallas_call(
        functools.partial(open_kernel, planes, step_j),
        grid=(n_j // step_j,),
        in_specs=[block, block, whole(gate_weight), whole(first_factor)],
        out_specs=[part] * planes,
        out_shape=[jax.ShapeDtypeStruct((n_i // planes, n_j, lanes, width), BF16)] * planes,
        scratch_shapes=[pltpu.VMEM((HEADS, n_i * lanes, n_i * lanes), BF16)],
        cost_estimate=pl.CostEstimate(
            flops=2 * count * (width + n_i * lanes), bytes_accessed=6 * count, transcendentals=count
        ),
        name="open_side",
    )(tokens, cotangent, gate_weight, first_factor)


def moved_last(factor, part):
    moved = place(factor.shape[0], part).astype(BF16)
    return dot_rows(dot(moved, factor).astype(BF16), moved).astype(BF16)


def forward_kernel(planes, b_ref, c_ref, *refs):
    x_refs, y_refs = refs[:planes], refs[planes : 2 * planes]
    bx_ref, wide = refs[2 * planes :]
    groups, pair_y, n_j, lanes, size = x_refs[0].shape
    part = pair_y * lanes
    last = moved_last(b_ref[0], part)
    wide[...] = spread(c_ref[0], lanes)

    def over_last(t, carry):
        g, j = t // (n_j // 2), (t % (n_j // 2)) * 2
        pair = [
            jnp.concatenate([ref[g, :, j + p].reshape(part, size) for ref in x_refs], axis=0) for p in range(2)
        ]
        out = dot(last, jnp.concatenate(pair, axis=1)).astype(BF16)
        for m in range(planes):
            for p in range(2):
                piece = out[m * part : (m + 1) * part, p * size : (p + 1) * size]
                bx_ref[m, g, :, j + p] = piece.reshape(pair_y, lanes, size)
        return carry

    lax.fori_loop(0, groups * n_j // 2, over_last, 0, unroll=2)
    for m in range(planes):
        held = [bx_ref[m, :, y].reshape(groups * n_j * lanes, size) for y in range(pair_y)]
        out = dot(wide[...], jnp.concatenate(held, axis=1)).astype(BF16)
        for y in range(pair_y):
            y_refs[m][:, y] = out[:, y * size : (y + 1) * size].reshape(groups, n_j, lanes, size)


def forward_side(values, last_factor, middle_factor):
    planes = len(values)
    groups, pair_y, n_j, lanes, width = values[0].shape
    size, n_middle = width // HEADS, groups * n_j
    block = pl.BlockSpec((groups, pair_y, n_j, lanes, size), lambda h: (0, 0, 0, 0, h))
    one = lambda a: pl.BlockSpec((1,) + a.shape[1:], lambda h: (h, 0, 0))
    count = values[0].size * planes
    shape = jax.ShapeDtypeStruct(values[0].shape, BF16)
    return pl.pallas_call(
        functools.partial(forward_kernel, planes),
        grid=(HEADS,),
        in_specs=[one(last_factor), one(middle_factor)] + [block] * planes,
        out_specs=[block] * planes
        + [pl.BlockSpec((planes, groups, pair_y, n_j, lanes, size), lambda h: (0, 0, 0, 0, 0, h))],
        out_shape=[shape] * planes + [jax.ShapeDtypeStruct((planes,) + values[0].shape, BF16)],
        scratch_shapes=[pltpu.VMEM((n_middle * lanes, n_middle * lanes), BF16)],
        cost_estimate=pl.CostEstimate(
            flops=2 * count * (n_middle * lanes + last_factor.shape[1]),
            bytes_accessed=6 * count,
            transcendentals=0,
        ),
        name="forward_side",
    )(last_factor, middle_factor, *values)


def backward_kernel(planes, b_ref, c_ref, bx_ref, *refs):
    x_refs, v_refs, u_refs = (refs[n * planes : (n + 1) * planes] for n in range(3))
    gl_ref, gm_ref, sent_all, cv, acc, wide = refs[3 * planes :]
    groups, pair_y, n_j, lanes, size = x_refs[0].shape
    rows, part = groups * n_j * lanes, pair_y * lanes
    wide[...] = spread(c_ref[0], lanes, turned=True)
    acc[...] = jnp.zeros_like(acc)
    for m in range(planes):
        sent_all[m] = v_refs[m][...]

    def over_middle(m, carry):
        sent = jnp.concatenate([sent_all[m, :, y].reshape(rows, size) for y in range(pair_y)], axis=1)
        held = jnp.concatenate([bx_ref[m, :, y].reshape(rows, size) for y in range(pair_y)], axis=1)
        acc[...] += dot_rows(sent, held)
        out = dot(wide[...], sent).astype(BF16)
        for y in range(pair_y):
            cv[m, :, y] = out[:, y * size : (y + 1) * size].reshape(groups, n_j, lanes, size)
        return carry

    lax.fori_loop(0, planes, over_middle, 0)
    gm_ref[0] = gather_diagonal(acc[...], groups * n_j, lanes)
    last = moved_last(b_ref[0], part)

    def over_last(t, total):
        g, j = t // (n_j // 2), (t % (n_j // 2)) * 2
        back, held = [
            jnp.concatenate(
                [
                    jnp.concatenate([ref[g, :, j + p].reshape(part, size) for ref in group], axis=0)
                    for p in range(2)
                ],
                axis=1,
            )
            for group in ([cv.at[m] for m in range(planes)], x_refs)
        ]
        out = dot(last, back).astype(BF16)
        for m in range(planes):
            for p in range(2):
                piece = out[m * part : (m + 1) * part, p * size : (p + 1) * size]
                u_refs[m][g, :, j + p] = piece.reshape(pair_y, lanes, size)
        return total + dot_rows(back, held)

    n_last = planes * part
    total = lax.fori_loop(0, groups * n_j // 2, over_last, jnp.zeros((n_last, n_last), F32), unroll=2)
    moved = place(n_last, part)
    gl_ref[0] = exact(exact(moved, total), moved)


def backward_side(sent, values, mixed, last_factor_t, middle_factor):
    planes = len(values)
    groups, pair_y, n_j, lanes, width = values[0].shape
    size, n_middle, n_last = width // HEADS, groups * n_j, last_factor_t.shape[1]
    block = pl.BlockSpec((groups, pair_y, n_j, lanes, size), lambda h: (0, 0, 0, 0, h))
    every = (planes, groups, pair_y, n_j, lanes, size)
    one = lambda n: pl.BlockSpec((1, n, n), lambda h: (h, 0, 0))
    count = values[0].size * planes
    wide = n_middle * lanes
    return pl.pallas_call(
        functools.partial(backward_kernel, planes),
        grid=(HEADS,),
        in_specs=[one(n_last), one(n_middle), pl.BlockSpec(every, lambda h: (0, 0, 0, 0, 0, h))]
        + [block] * (2 * planes),
        out_specs=[block] * planes + [one(n_last), one(n_middle)],
        out_shape=[jax.ShapeDtypeStruct(values[0].shape, BF16)] * planes
        + [
            jax.ShapeDtypeStruct((HEADS, n_last, n_last), F32),
            jax.ShapeDtypeStruct((HEADS, n_middle, n_middle), F32),
        ],
        scratch_shapes=[
            pltpu.VMEM(every, BF16),
            pltpu.VMEM(every, BF16),
            pltpu.VMEM((wide, wide), F32),
            pltpu.VMEM((wide, wide), BF16),
        ],
        cost_estimate=pl.CostEstimate(
            flops=4 * count * (wide + n_last), bytes_accessed=8 * count, transcendentals=0
        ),
        name="backward_side",
    )(last_factor_t, middle_factor, mixed, *values, *sent)


def close_kernel(planes, step_j, x_ref, g_ref, w_ref, a_ref, *refs):
    y_refs = refs[:planes]
    t_ref, gg_ref, gf_ref, acc, wide = refs[planes:]
    n_i, _, lanes, width = x_ref.shape
    size, rows_n = width // HEADS, n_i * lanes
    part = n_i // planes

    @pl.when(pl.program_id(0) == 0)
    def _():
        acc[...] = jnp.zeros_like(acc)
        gg_ref[...] = jnp.zeros_like(gg_ref)
        moved = place(n_i, part).astype(BF16)
        for h in range(HEADS):
            wide[h] = spread(dot_rows(a_ref[h], moved).astype(BF16), lanes)

    rows, ups, gates, mixes, sent = [], [], [], [], []
    for j in range(step_j):
        rows.append(x_ref[:, j].reshape(rows_n, width))
        ups.append(g_ref[:, j].reshape(rows_n, width).astype(F32))
        gates.append(gate_of(rows[j], w_ref[...]))
        mixes.append(jnp.concatenate([ref[:, j].reshape(part * lanes, width) for ref in y_refs], axis=0))
        sent.append((ups[j] * gates[j]).astype(BF16))
    outs = []
    for h in range(HEADS):
        cut = slice(h * size, (h + 1) * size)
        held = jnp.concatenate([m[:, cut] for m in mixes], axis=1)
        back = jnp.concatenate([d[:, cut] for d in sent], axis=1)
        acc[h] += dot_rows(back, held)
        outs.append(dot(wide[h], held).astype(BF16).astype(F32))
    for j in range(step_j):
        mixer = jnp.concatenate([o[:, j * size : (j + 1) * size] for o in outs], axis=1)
        d_pre = (ups[j] * mixer * gates[j] * (1.0 - gates[j])).astype(BF16)
        t_ref[:, j] = dot_rows(d_pre, w_ref[...]).astype(BF16).reshape(n_i, lanes, width)
        gg_ref[...] += lax.dot_general(
            rows[j], d_pre, (((0,), (0,)), ((), ())), preferred_element_type=F32
        )

    @pl.when(pl.program_id(0) == pl.num_programs(0) - 1)
    def _():
        for h in range(HEADS):
            gf_ref[h] = exact(gather_diagonal(acc[h], n_i, lanes), place(n_i, part))


def close_side(tokens, cotangent, mixed, gate_weight, first_factor):
    planes = len(mixed)
    n_i, n_j, lanes, width = tokens.shape
    step_j = 2
    block = pl.BlockSpec((n_i, step_j, lanes, width), lambda j: (0, j, 0, 0))
    part = pl.BlockSpec((n_i // planes, step_j, lanes, width), lambda j: (0, j, 0, 0))
    whole = lambda shape: pl.BlockSpec(shape, lambda j: (0,) * len(shape))
    count = tokens.size
    return pl.pallas_call(
        functools.partial(close_kernel, planes, step_j),
        grid=(n_j // step_j,),
        in_specs=[block, block, whole(gate_weight.shape), whole(first_factor.shape)] + [part] * planes,
        out_specs=[block, whole((width, width)), whole((HEADS, n_i, n_i))],
        out_shape=[
            jax.ShapeDtypeStruct(tokens.shape, BF16),
            jax.ShapeDtypeStruct((width, width), F32),
            jax.ShapeDtypeStruct((HEADS, n_i, n_i), F32),
        ],
        scratch_shapes=[
            pltpu.VMEM((HEADS, n_i * lanes, n_i * lanes), F32),
            pltpu.VMEM((HEADS, n_i * lanes, n_i * lanes), BF16),
        ],
        cost_estimate=pl.CostEstimate(
            flops=2 * count * (3 * width + 2 * n_i * lanes),
            bytes_accessed=8 * count,
            transcendentals=count,
        ),
        name="close_side",
    )(tokens, cotangent, gate_weight, first_factor, *mixed)


def finish_kernel(z_ref, b_ref, t_ref, *refs):
    refs[-1][...] = (b_ref[...].astype(F32) + t_ref[...].astype(F32)).astype(BF16)


def finish(back, gate_term, m, held=None):
    part, n_j, lanes, width = back.shape
    step = part // 4
    here = pl.BlockSpec((step, n_j, lanes, width), lambda t, z: (t, 0, 0, 0))
    there = pl.BlockSpec((step, n_j, lanes, width), lambda t, z: ((z[0] ^ m) * 4 + t, 0, 0, 0))
    more = [] if held is None else [held]
    return pl.pallas_call(
        finish_kernel,
        grid_spec=pltpu.PrefetchScalarGridSpec(
            num_scalar_prefetch=1,
            grid=(4,),
            in_specs=[here, there] + [pl.BlockSpec(memory_space=pl.ANY)] * len(more),
            out_specs=there,
        ),
        out_shape=jax.ShapeDtypeStruct(gate_term.shape, BF16),
        input_output_aliases={3: 0} if more else {},
        cost_estimate=pl.CostEstimate(flops=back.size, bytes_accessed=6 * back.size, transcendentals=0),
    )(lax.axis_index("z").reshape(1), back, gate_term, *more)


def over_z(part, m):
    if m == 0:
        return part
    pairs = [(z, z ^ m) for z in range(lax.axis_size("z"))]
    return lax.ppermute(part, "z", pairs)


def in_plane(part):
    return lax.all_to_all(part, ("grp", "y"), split_axis=0, concat_axis=0, tiled=True)


def shifted(parts, axis):
    count = lax.axis_size(axis)
    me = lax.axis_index(axis)
    out = []
    for d in range(1, count):
        part = lax.dynamic_index_in_dim(parts, (me + d) % count, 0, False)
        out.append(lax.ppermute(part, axis, [(i, (i + d) % count) for i in range(count)]))
    return out


def share_kernel(factor, *refs):
    total = refs[0][...]
    for part in refs[1:-1]:
        total += part[...]
    refs[-1][...] = total * factor


def share_sum(parts, factor):
    return pl.pallas_call(
        functools.partial(share_kernel, factor),
        out_shape=jax.ShapeDtypeStruct(parts[0].shape, F32),
        name="share_sum",
    )(*parts)


def ordered_kernel(axis, *refs):
    parts, out_ref, held = refs[:-2], refs[-2], refs[-1]
    count = len(parts)
    me = lax.axis_index(axis)
    for d, part in enumerate(parts):
        held[d] = part[...]
    total = held[lax.rem(me + count, count)]
    for source in range(1, count):
        total += held[lax.rem(me - source + count, count)]
    out_ref[...] = total


def ordered_sum(parts, axis):
    shape = parts[0].shape
    return pl.pallas_call(
        functools.partial(ordered_kernel, axis),
        out_shape=jax.ShapeDtypeStruct(shape, F32),
        scratch_shapes=[pltpu.VMEM((len(parts),) + shape, F32)],
        name="ordered_sum",
    )(*parts)


def reduced_direct(gate_part, first_part, middle_part, last_part, factor):
    groups, blocks = lax.axis_size("grp"), lax.axis_size(PLANES)
    width = gate_part.shape[0]
    n_last, n_middle, n_first = last_part.shape[1], middle_part.shape[1], first_part.shape[1]
    lane = width // groups
    own = HEADS // groups

    def flat(parts):
        return parts.reshape(parts.shape[0], -1, lane)

    packed = jnp.concatenate(
        [
            gate_part.reshape(width, groups, lane).transpose(1, 0, 2),
            flat(last_part.reshape(groups, -1)),
            flat(middle_part.reshape(HEADS, groups, -1).transpose(1, 0, 2)),
            flat(first_part.reshape(groups, -1)),
        ],
        axis=1,
    )
    mine = lax.dynamic_index_in_dim(packed, lax.axis_index("grp"), 0, False)
    share = share_sum([mine] + shifted(packed, "grp"), factor)
    cuts = [width, own * n_last * n_last // lane, HEADS * n_middle * n_middle // groups // lane]
    gate, last, middle, first = jnp.split(share, [sum(cuts[: n + 1]) for n in range(3)])
    last = last.reshape(own, blocks, n_last // blocks, n_last).transpose(1, 0, 2, 3)
    again = jnp.concatenate(
        [
            gate.reshape(blocks, -1, lane),
            flat(last.reshape(blocks, -1)),
            jnp.broadcast_to(middle, (blocks,) + middle.shape),
            jnp.broadcast_to(first, (blocks,) + first.shape),
        ],
        axis=1,
    )
    mine = lax.dynamic_index_in_dim(again, lax.axis_index(PLANES), 0, False)
    total = ordered_sum([mine] + shifted(again, PLANES), PLANES)
    cuts = [width // blocks, own * n_last * n_last // blocks // lane, middle.shape[0]]
    gate, last, middle, first = jnp.split(total, [sum(cuts[: n + 1]) for n in range(3)])
    give = jnp.concatenate([gate, last, first])
    me = lax.axis_index("grp")
    spread_out = jnp.zeros((groups,) + give.shape, F32)
    spread_out = lax.dynamic_update_index_in_dim(spread_out, give, me, 0)
    for d, part in enumerate(shifted(jnp.broadcast_to(give, (groups,) + give.shape), "grp"), 1):
        spread_out = lax.dynamic_update_index_in_dim(spread_out, part, (me - d) % groups, 0)
    gate, last, first = jnp.split(spread_out, [gate.shape[0], gate.shape[0] + last.shape[0]], axis=1)
    return (
        gate.transpose(1, 0, 2).reshape(-1, width),
        first.reshape(HEADS, n_first, n_first),
        middle.reshape(HEADS, n_middle // groups, n_middle),
        last.reshape(HEADS, n_last // blocks, n_last),
    )


def ordered(tokens, cotangent, gate_weight, first_factor, middle_factor, last_factor):
    groups, planes, pair_y = (lax.axis_size(axis) for axis in ("grp", "z", "y"))
    part = tokens.shape[0] // planes
    split = (groups, pair_y) + tokens.shape[1:]
    home = (part,) + tokens.shape[1:]
    z = lax.axis_index("z")
    held = [lax.dynamic_slice_in_dim(tokens, (z ^ m) * part, part, 0) for m in range(planes)]
    at_whole = [in_plane(over_z(held[m], m)).reshape(split) for m in range(planes)]
    sent = open_side(tokens, cotangent, gate_weight, first_factor, planes)
    sent_whole = [over_z(in_plane(sent[m]), m).reshape(split) for m in range(planes)]
    *forward, mixed = forward_side(at_whole, last_factor, middle_factor)
    forward_home = [over_z(in_plane(forward[m].reshape(home)), m) for m in range(planes)]
    *backward, last_part, middle_part = backward_side(
        sent_whole, at_whole, mixed, last_factor.transpose(0, 2, 1), middle_factor
    )
    back_home = [over_z(in_plane(backward[m].reshape(home)), m) for m in range(planes)]
    gate_term, gate_part, first_part = close_side(
        tokens, cotangent, forward_home, gate_weight, first_factor
    )
    sums = reduced_direct(
        gate_part, first_part, middle_part, last_part, 1.0 / math.sqrt(positions(tokens, PLANES))
    )
    d_tokens = None
    for m in range(planes):
        d_tokens = finish(back_home[m], gate_term, m, d_tokens)
    return (d_tokens,) + sums


def direct(*arrays):
    return ordered(*arrays)


def fits(shape, groups, blocks):
    n_i, n_j, lanes, width = shape
    planes = blocks // 2
    return (
        n_i == groups * blocks
        and blocks == 2 * planes
        and planes & (planes - 1) == 0
        and n_i % (4 * planes) == 0
        and lanes % 16 == 0
        and n_j % 2 == 0
        and width == groups * 128
        and HEADS % groups == 0
        and width % (HEADS * 128) == 0
    )


def shards_of(mesh, tokens):
    groups, blocks = mesh.shape["grp"], mesh.shape["seq"]
    n_i, n_j, n_k, width = tokens.shape
    if fits((n_i, n_j // groups, n_k // blocks, width), groups, blocks):
        devices = mesh.devices.reshape(groups, blocks // 2, 2)
        return direct, jax.sharding.Mesh(devices, ("grp",) + PLANES), PLANES
    return general, mesh, "seq"


def solution(mesh):
    def step(*arrays):
        body, fine, seq = shards_of(mesh, arrays[0])
        spread_in = P(None, "grp", seq, None)
        in_specs = (spread_in, spread_in, P(), P(), P(), P())
        out_specs = (spread_in, P(seq, None), P(), P(None, "grp", None), P(None, seq, None))
        return jax.shard_map(body, mesh=fine, in_specs=in_specs, out_specs=out_specs, check_vma=False)(*arrays)

    return step
```

```python
import functools
import math

import jax
import jax.numpy as jnp
from jax import lax
from jax.experimental import pallas as pl
from jax.experimental.pallas import tpu as pltpu
from jax.sharding import PartitionSpec as P


HEADS = 4
F32 = jnp.float32
BF16 = jnp.bfloat16


def headed(values):
    return values.reshape(values.shape[:-1] + (HEADS, values.shape[-1] // HEADS))


def mixing(weights, values, form):
    result = jnp.einsum(form, weights, headed(values), preferred_element_type=F32)
    return result.reshape(values.shape)


def contract(left, right, form):
    return jnp.einsum(form, headed(left), headed(right), preferred_element_type=F32)


def send_last(values):
    return lax.all_to_all(values, "seq", split_axis=0, concat_axis=2, tiled=True)


def send_middle(values):
    return lax.all_to_all(values, "grp", split_axis=2, concat_axis=1, tiled=True)


def return_middle(values):
    return lax.all_to_all(values, "grp", split_axis=1, concat_axis=2, tiled=True)


def return_last(values):
    return lax.all_to_all(values, "seq", split_axis=2, concat_axis=0, tiled=True)


def positions(tokens, seq):
    return math.prod(tokens.shape[:3]) * lax.axis_size("grp") * lax.axis_size(seq)


def general(tokens, cotangent, gate_weight, first_factor, middle_factor, last_factor):
    width = tokens.shape[-1]
    rows = tokens.reshape(-1, width)
    gate = jax.nn.sigmoid(jnp.dot(rows, gate_weight, preferred_element_type=F32))
    gate = gate.reshape(tokens.shape)
    first_out = mixing(first_factor, tokens, "hab,bjkhe->ajkhe").astype(BF16)
    last_in = send_last(first_out)
    last_out = mixing(last_factor, last_in, "hab,ijbhe->ijahe").astype(BF16)
    middle_in = send_middle(last_out)
    middle_out = mixing(middle_factor, middle_in, "hab,ibkhe->iakhe").astype(BF16)
    mixer = return_last(return_middle(middle_out))
    upstream = cotangent.astype(F32)
    d_mix = (upstream * gate).astype(BF16)
    d_pre = (upstream * mixer.astype(F32) * gate * (1.0 - gate)).astype(BF16)
    pre_rows = d_pre.reshape(-1, width)
    gate_part = jnp.einsum("tc,td->cd", rows, pre_rows, preferred_element_type=F32)
    gate_term = jnp.einsum("td,cd->tc", pre_rows, gate_weight, preferred_element_type=F32)
    middle_grad_in = send_middle(send_last(d_mix))
    middle_back = mixing(middle_factor, middle_grad_in, "hba,ibkhe->iakhe").astype(BF16)
    middle_part = contract(middle_grad_in, middle_in, "iakhe,ibkhe->hab")
    last_back_in = return_middle(middle_back)
    last_back = mixing(last_factor, last_back_in, "hba,ijbhe->ijahe").astype(BF16)
    last_part = contract(last_back_in, last_in, "ijahe,ijbhe->hab")
    first_back_in = return_last(last_back)
    first_back = mixing(first_factor, first_back_in, "hba,bjkhe->ajkhe")
    first_part = contract(first_back_in, tokens, "ajkhe,bjkhe->hab")
    d_tokens = (first_back.reshape(-1, width) + gate_term).astype(BF16).reshape(tokens.shape)
    return (d_tokens,) + reduced(
        gate_part, first_part, middle_part, last_part, 1.0 / math.sqrt(positions(tokens, "seq"))
    )


def reduced(gate_part, first_part, middle_part, last_part, factor):
    gate_share = lax.psum_scatter(gate_part, "seq", scatter_dimension=0, tiled=True)
    last_share = lax.psum_scatter(last_part, "seq", scatter_dimension=1, tiled=True)
    middle_share = lax.psum_scatter(middle_part, "grp", scatter_dimension=1, tiled=True)
    gate_sum, last_sum, first_half = lax.psum((gate_share, last_share, first_part), "grp")
    middle_sum, first_sum = lax.psum((middle_share, first_half), "seq")
    return gate_sum * factor, first_sum * factor, middle_sum * factor, last_sum * factor


PLANES = ("z", "y")


def dot(left, right):
    return jnp.dot(left, right, preferred_element_type=F32)


def dot_rows(left, right):
    return lax.dot_general(left, right, (((1,), (1,)), ((), ())), preferred_element_type=F32)


def exact(left, right):
    return jnp.dot(left, right, precision=lax.Precision.HIGHEST, preferred_element_type=F32)


def iota(shape, axis):
    return lax.broadcasted_iota(jnp.int32, shape, axis)


def place(size, block):
    source = ((iota((size, size), 0) // block) ^ lax.axis_index("z")) * block + iota((size, size), 0) % block
    return jnp.where(source == iota((size, size), 1), 1.0, 0.0)


def spread(factor, lanes, turned=False):
    size = factor.shape[0]
    wide = size * lanes
    tall = jnp.where(iota((wide, size), 0) // lanes == iota((wide, size), 1), 1.0, 0.0).astype(BF16)
    flat = jnp.where(iota((size, wide), 1) // lanes == iota((size, wide), 0), 1.0, 0.0).astype(BF16)
    picked = (dot_rows if turned else dot)(tall, factor).astype(BF16)
    same = iota((wide, wide), 0) % lanes == iota((wide, wide), 1) % lanes
    return jnp.where(same, dot(picked, flat), 0.0).astype(BF16)


def gather_diagonal(total, size, lanes):
    wide = size * lanes
    same = iota((wide, wide), 0) % lanes == iota((wide, wide), 1) % lanes
    kept = jnp.where(same, total, 0.0).reshape(size, lanes, wide).sum(axis=1)
    collect = jnp.where(iota((wide, size), 0) // lanes == iota((wide, size), 1), 1.0, 0.0)
    return exact(kept, collect)


def gate_of(rows, weight):
    return jax.nn.sigmoid(dot(rows, weight))


def open_kernel(planes, step_j, x_ref, g_ref, w_ref, a_ref, *refs):
    v_refs, wide = refs[:planes], refs[planes]
    n_i, _, lanes, width = x_ref.shape
    size, part = width // HEADS, n_i // planes

    @pl.when(pl.program_id(0) == 0)
    def _():
        moved = place(n_i, part).astype(BF16)
        for h in range(HEADS):
            wide[h] = spread(dot_rows(a_ref[h], moved).astype(BF16), lanes, turned=True)

    sent = []
    for j in range(step_j):
        rows = x_ref[:, j].reshape(n_i * lanes, width)
        up = g_ref[:, j].reshape(n_i * lanes, width).astype(F32)
        sent.append((up * gate_of(rows, w_ref[...])).astype(BF16))
    for h in range(HEADS):
        pair = jnp.concatenate([d[:, h * size : (h + 1) * size] for d in sent], axis=1)
        out = dot(wide[h], pair).astype(BF16)
        for m in range(planes):
            for j in range(step_j):
                piece = out[m * part * lanes : (m + 1) * part * lanes, j * size : (j + 1) * size]
                v_refs[m][:, j, :, h * size : (h + 1) * size] = piece.reshape(part, lanes, size)


def open_side(tokens, cotangent, gate_weight, first_factor, planes):
    n_i, n_j, lanes, width = tokens.shape
    step_j = 2
    block = pl.BlockSpec((n_i, step_j, lanes, width), lambda j: (0, j, 0, 0))
    part = pl.BlockSpec((n_i // planes, step_j, lanes, width), lambda j: (0, j, 0, 0))
    whole = lambda a: pl.BlockSpec(a.shape, lambda j: (0,) * a.ndim)
    count = tokens.size
    return pl.pallas_call(
        functools.partial(open_kernel, planes, step_j),
        grid=(n_j // step_j,),
        in_specs=[block, block, whole(gate_weight), whole(first_factor)],
        out_specs=[part] * planes,
        out_shape=[jax.ShapeDtypeStruct((n_i // planes, n_j, lanes, width), BF16)] * planes,
        scratch_shapes=[pltpu.VMEM((HEADS, n_i * lanes, n_i * lanes), BF16)],
        cost_estimate=pl.CostEstimate(
            flops=2 * count * (width + n_i * lanes), bytes_accessed=6 * count, transcendentals=count
        ),
        name="open_side",
    )(tokens, cotangent, gate_weight, first_factor)


def moved_last(factor, part):
    moved = place(factor.shape[0], part).astype(BF16)
    return dot_rows(dot(moved, factor).astype(BF16), moved).astype(BF16)


def forward_kernel(planes, b_ref, c_ref, *refs):
    x_refs, y_refs = refs[:planes], refs[planes : 2 * planes]
    bx_ref, wide = refs[2 * planes :]
    groups, pair_y, n_j, lanes, size = x_refs[0].shape
    part = pair_y * lanes
    last = moved_last(b_ref[0], part)
    wide[...] = spread(c_ref[0], lanes)

    def over_last(t, carry):
        g, j = t // (n_j // 2), (t % (n_j // 2)) * 2
        pair = [
            jnp.concatenate([ref[g, :, j + p].reshape(part, size) for ref in x_refs], axis=0) for p in range(2)
        ]
        out = dot(last, jnp.concatenate(pair, axis=1)).astype(BF16)
        for m in range(planes):
            for p in range(2):
                piece = out[m * part : (m + 1) * part, p * size : (p + 1) * size]
                bx_ref[m, g, :, j + p] = piece.reshape(pair_y, lanes, size)
        return carry

    lax.fori_loop(0, groups * n_j // 2, over_last, 0, unroll=2)
    for m in range(planes):
        held = [bx_ref[m, :, y].reshape(groups * n_j * lanes, size) for y in range(pair_y)]
        out = dot(wide[...], jnp.concatenate(held, axis=1)).astype(BF16)
        for y in range(pair_y):
            y_refs[m][:, y] = out[:, y * size : (y + 1) * size].reshape(groups, n_j, lanes, size)


def forward_side(values, last_factor, middle_factor):
    planes = len(values)
    groups, pair_y, n_j, lanes, width = values[0].shape
    size, n_middle = width // HEADS, groups * n_j
    block = pl.BlockSpec((groups, pair_y, n_j, lanes, size), lambda h: (0, 0, 0, 0, h))
    one = lambda a: pl.BlockSpec((1,) + a.shape[1:], lambda h: (h, 0, 0))
    count = values[0].size * planes
    shape = jax.ShapeDtypeStruct(values[0].shape, BF16)
    return pl.pallas_call(
        functools.partial(forward_kernel, planes),
        grid=(HEADS,),
        in_specs=[one(last_factor), one(middle_factor)] + [block] * planes,
        out_specs=[block] * planes
        + [pl.BlockSpec((planes, groups, pair_y, n_j, lanes, size), lambda h: (0, 0, 0, 0, 0, h))],
        out_shape=[shape] * planes + [jax.ShapeDtypeStruct((planes,) + values[0].shape, BF16)],
        scratch_shapes=[pltpu.VMEM((n_middle * lanes, n_middle * lanes), BF16)],
        cost_estimate=pl.CostEstimate(
            flops=2 * count * (n_middle * lanes + last_factor.shape[1]),
            bytes_accessed=6 * count,
            transcendentals=0,
        ),
        name="forward_side",
    )(last_factor, middle_factor, *values)


def backward_kernel(planes, b_ref, c_ref, bx_ref, *refs):
    x_refs, v_refs, u_refs = (refs[n * planes : (n + 1) * planes] for n in range(3))
    gl_ref, gm_ref, sent_all, cv, acc, wide = refs[3 * planes :]
    groups, pair_y, n_j, lanes, size = x_refs[0].shape
    rows, part = groups * n_j * lanes, pair_y * lanes
    wide[...] = spread(c_ref[0], lanes, turned=True)
    acc[...] = jnp.zeros_like(acc)
    for m in range(planes):
        sent_all[m] = v_refs[m][...]

    def over_middle(m, carry):
        sent = jnp.concatenate([sent_all[m, :, y].reshape(rows, size) for y in range(pair_y)], axis=1)
        held = jnp.concatenate([bx_ref[m, :, y].reshape(rows, size) for y in range(pair_y)], axis=1)
        acc[...] += dot_rows(sent, held)
        out = dot(wide[...], sent).astype(BF16)
        for y in range(pair_y):
            cv[m, :, y] = out[:, y * size : (y + 1) * size].reshape(groups, n_j, lanes, size)
        return carry

    lax.fori_loop(0, planes, over_middle, 0)
    gm_ref[0] = gather_diagonal(acc[...], groups * n_j, lanes)
    last = moved_last(b_ref[0], part)

    def over_last(t, total):
        g, j = t // (n_j // 2), (t % (n_j // 2)) * 2
        back, held = [
            jnp.concatenate(
                [
                    jnp.concatenate([ref[g, :, j + p].reshape(part, size) for ref in group], axis=0)
                    for p in range(2)
                ],
                axis=1,
            )
            for group in ([cv.at[m] for m in range(planes)], x_refs)
        ]
        out = dot(last, back).astype(BF16)
        for m in range(planes):
            for p in range(2):
                piece = out[m * part : (m + 1) * part, p * size : (p + 1) * size]
                u_refs[m][g, :, j + p] = piece.reshape(pair_y, lanes, size)
        return total + dot_rows(back, held)

    n_last = planes * part
    total = lax.fori_loop(0, groups * n_j // 2, over_last, jnp.zeros((n_last, n_last), F32), unroll=2)
    moved = place(n_last, part)
    gl_ref[0] = exact(exact(moved, total), moved)


def backward_side(sent, values, mixed, last_factor_t, middle_factor):
    planes = len(values)
    groups, pair_y, n_j, lanes, width = values[0].shape
    size, n_middle, n_last = width // HEADS, groups * n_j, last_factor_t.shape[1]
    block = pl.BlockSpec((groups, pair_y, n_j, lanes, size), lambda h: (0, 0, 0, 0, h))
    every = (planes, groups, pair_y, n_j, lanes, size)
    one = lambda n: pl.BlockSpec((1, n, n), lambda h: (h, 0, 0))
    count = values[0].size * planes
    wide = n_middle * lanes
    return pl.pallas_call(
        functools.partial(backward_kernel, planes),
        grid=(HEADS,),
        in_specs=[one(n_last), one(n_middle), pl.BlockSpec(every, lambda h: (0, 0, 0, 0, 0, h))]
        + [block] * (2 * planes),
        out_specs=[block] * planes + [one(n_last), one(n_middle)],
        out_shape=[jax.ShapeDtypeStruct(values[0].shape, BF16)] * planes
        + [
            jax.ShapeDtypeStruct((HEADS, n_last, n_last), F32),
            jax.ShapeDtypeStruct((HEADS, n_middle, n_middle), F32),
        ],
        scratch_shapes=[
            pltpu.VMEM(every, BF16),
            pltpu.VMEM(every, BF16),
            pltpu.VMEM((wide, wide), F32),
            pltpu.VMEM((wide, wide), BF16),
        ],
        cost_estimate=pl.CostEstimate(
            flops=4 * count * (wide + n_last), bytes_accessed=8 * count, transcendentals=0
        ),
        name="backward_side",
    )(last_factor_t, middle_factor, mixed, *values, *sent)


def close_kernel(planes, step_j, x_ref, g_ref, w_ref, a_ref, *refs):
    y_refs = refs[:planes]
    t_ref, gg_ref, gf_ref, acc, wide = refs[planes:]
    n_i, _, lanes, width = x_ref.shape
    size, rows_n = width // HEADS, n_i * lanes
    part = n_i // planes

    @pl.when(pl.program_id(0) == 0)
    def _():
        acc[...] = jnp.zeros_like(acc)
        gg_ref[...] = jnp.zeros_like(gg_ref)
        moved = place(n_i, part).astype(BF16)
        for h in range(HEADS):
            wide[h] = spread(dot_rows(a_ref[h], moved).astype(BF16), lanes)

    rows, ups, gates, mixes, sent = [], [], [], [], []
    for j in range(step_j):
        rows.append(x_ref[:, j].reshape(rows_n, width))
        ups.append(g_ref[:, j].reshape(rows_n, width).astype(F32))
        gates.append(gate_of(rows[j], w_ref[...]))
        mixes.append(jnp.concatenate([ref[:, j].reshape(part * lanes, width) for ref in y_refs], axis=0))
        sent.append((ups[j] * gates[j]).astype(BF16))
    outs = []
    for h in range(HEADS):
        cut = slice(h * size, (h + 1) * size)
        held = jnp.concatenate([m[:, cut] for m in mixes], axis=1)
        back = jnp.concatenate([d[:, cut] for d in sent], axis=1)
        acc[h] += dot_rows(back, held)
        outs.append(dot(wide[h], held).astype(BF16).astype(F32))
    for j in range(step_j):
        mixer = jnp.concatenate([o[:, j * size : (j + 1) * size] for o in outs], axis=1)
        d_pre = (ups[j] * mixer * gates[j] * (1.0 - gates[j])).astype(BF16)
        t_ref[:, j] = dot_rows(d_pre, w_ref[...]).astype(BF16).reshape(n_i, lanes, width)
        gg_ref[...] += lax.dot_general(
            rows[j], d_pre, (((0,), (0,)), ((), ())), preferred_element_type=F32
        )

    @pl.when(pl.program_id(0) == pl.num_programs(0) - 1)
    def _():
        for h in range(HEADS):
            gf_ref[h] = exact(gather_diagonal(acc[h], n_i, lanes), place(n_i, part))


def close_side(tokens, cotangent, mixed, gate_weight, first_factor):
    planes = len(mixed)
    n_i, n_j, lanes, width = tokens.shape
    step_j = 2
    block = pl.BlockSpec((n_i, step_j, lanes, width), lambda j: (0, j, 0, 0))
    part = pl.BlockSpec((n_i // planes, step_j, lanes, width), lambda j: (0, j, 0, 0))
    whole = lambda shape: pl.BlockSpec(shape, lambda j: (0,) * len(shape))
    count = tokens.size
    return pl.pallas_call(
        functools.partial(close_kernel, planes, step_j),
        grid=(n_j // step_j,),
        in_specs=[block, block, whole(gate_weight.shape), whole(first_factor.shape)] + [part] * planes,
        out_specs=[block, whole((width, width)), whole((HEADS, n_i, n_i))],
        out_shape=[
            jax.ShapeDtypeStruct(tokens.shape, BF16),
            jax.ShapeDtypeStruct((width, width), F32),
            jax.ShapeDtypeStruct((HEADS, n_i, n_i), F32),
        ],
        scratch_shapes=[
            pltpu.VMEM((HEADS, n_i * lanes, n_i * lanes), F32),
            pltpu.VMEM((HEADS, n_i * lanes, n_i * lanes), BF16),
        ],
        cost_estimate=pl.CostEstimate(
            flops=2 * count * (3 * width + 2 * n_i * lanes),
            bytes_accessed=8 * count,
            transcendentals=count,
        ),
        name="close_side",
    )(tokens, cotangent, gate_weight, first_factor, *mixed)


def finish_kernel(z_ref, b_ref, t_ref, *refs):
    refs[-1][...] = (b_ref[...].astype(F32) + t_ref[...].astype(F32)).astype(BF16)


def finish(back, gate_term, m, held=None):
    part, n_j, lanes, width = back.shape
    step = part // 4
    here = pl.BlockSpec((step, n_j, lanes, width), lambda t, z: (t, 0, 0, 0))
    there = pl.BlockSpec((step, n_j, lanes, width), lambda t, z: ((z[0] ^ m) * 4 + t, 0, 0, 0))
    more = [] if held is None else [held]
    return pl.pallas_call(
        finish_kernel,
        grid_spec=pltpu.PrefetchScalarGridSpec(
            num_scalar_prefetch=1,
            grid=(4,),
            in_specs=[here, there] + [pl.BlockSpec(memory_space=pl.ANY)] * len(more),
            out_specs=there,
        ),
        out_shape=jax.ShapeDtypeStruct(gate_term.shape, BF16),
        input_output_aliases={3: 0} if more else {},
        cost_estimate=pl.CostEstimate(flops=back.size, bytes_accessed=6 * back.size, transcendentals=0),
    )(lax.axis_index("z").reshape(1), back, gate_term, *more)


def over_z(part, m):
    if m == 0:
        return part
    pairs = [(z, z ^ m) for z in range(lax.axis_size("z"))]
    return lax.ppermute(part, "z", pairs)


def in_plane(part):
    return lax.all_to_all(part, ("grp", "y"), split_axis=0, concat_axis=0, tiled=True)


def shifted(parts, axis):
    count = lax.axis_size(axis)
    me = lax.axis_index(axis)
    out = []
    for d in range(1, count):
        part = lax.dynamic_index_in_dim(parts, (me + d) % count, 0, False)
        out.append(lax.ppermute(part, axis, [(i, (i + d) % count) for i in range(count)]))
    return out


def ordered_kernel(axis, factor, *refs):
    parts, out_ref, held = refs[:-2], refs[-2], refs[-1]
    count = len(parts)
    me = lax.axis_index(axis)
    for d, part in enumerate(parts):
        held[d] = part[...]
    total = held[lax.rem(me + count, count)]
    for source in range(1, count):
        total += held[lax.rem(me - source + count, count)]
    out_ref[...] = total * factor


def ordered_sum(parts, axis, factor=1.0):
    shape = parts[0].shape
    return pl.pallas_call(
        functools.partial(ordered_kernel, axis, factor),
        out_shape=jax.ShapeDtypeStruct(shape, F32),
        scratch_shapes=[pltpu.VMEM((len(parts),) + shape, F32)],
    )(*parts)


def reduced_direct(gate_part, first_part, middle_part, last_part, factor):
    groups, planes, pair_y = (lax.axis_size(axis) for axis in ("grp", "z", "y"))
    blocks = planes * pair_y
    width = gate_part.shape[0]
    n_last, n_middle, n_first = last_part.shape[1], middle_part.shape[1], first_part.shape[1]
    lane = width // groups
    own = HEADS // groups

    def both(parts):
        parts = parts.reshape(groups, 1, -1, lane)
        return jnp.broadcast_to(parts, (groups, pair_y) + parts.shape[2:])

    gate = gate_part.reshape(planes, pair_y, -1, groups, lane).transpose(3, 1, 0, 2, 4)
    last = last_part.reshape(groups, own, planes, pair_y, -1).transpose(0, 3, 2, 1, 4)
    packed = jnp.concatenate(
        [
            gate.reshape(groups, pair_y, -1, lane),
            last.reshape(groups, pair_y, -1, lane),
            both(middle_part.reshape(HEADS, groups, -1).transpose(1, 0, 2)),
            both(first_part),
        ],
        axis=2,
    )
    packed = packed.reshape((groups * pair_y,) + packed.shape[2:])
    plane = ("grp", "y")
    mine = lax.dynamic_index_in_dim(packed, lax.axis_index(plane), 0, False)
    share = ordered_sum([mine] + shifted(packed, plane), plane, factor)
    cuts = [width // pair_y, own * n_last * n_last // pair_y // lane, HEADS * n_middle * n_middle // groups // lane]
    gate, last, middle, first = jnp.split(share, [sum(cuts[: n + 1]) for n in range(3)])
    again = jnp.concatenate(
        [
            gate.reshape(planes, -1, lane),
            last.reshape(planes, -1, lane),
            jnp.broadcast_to(middle, (planes,) + middle.shape),
            jnp.broadcast_to(first, (planes,) + first.shape),
        ],
        axis=1,
    )
    mine = lax.dynamic_index_in_dim(again, lax.axis_index("z"), 0, False)
    total = ordered_sum([mine] + shifted(again, "z"), "z")
    cuts = [width // blocks, own * n_last * n_last // blocks // lane, middle.shape[0]]
    gate, last, middle, first = jnp.split(total, [sum(cuts[: n + 1]) for n in range(3)])
    give = jnp.concatenate([gate, last, first])
    me = lax.axis_index("grp")
    spread_out = jnp.zeros((groups,) + give.shape, F32)
    spread_out = lax.dynamic_update_index_in_dim(spread_out, give, me, 0)
    for d, part in enumerate(shifted(jnp.broadcast_to(give, (groups,) + give.shape), "grp"), 1):
        spread_out = lax.dynamic_update_index_in_dim(spread_out, part, (me - d) % groups, 0)
    gate, last, first = jnp.split(spread_out, [gate.shape[0], gate.shape[0] + last.shape[0]], axis=1)
    return (
        gate.transpose(1, 0, 2).reshape(-1, width),
        first.reshape(HEADS, n_first, n_first),
        middle.reshape(HEADS, n_middle // groups, n_middle),
        last.reshape(HEADS, n_last // blocks, n_last),
    )


def ordered(tokens, cotangent, gate_weight, first_factor, middle_factor, last_factor):
    groups, planes, pair_y = (lax.axis_size(axis) for axis in ("grp", "z", "y"))
    part = tokens.shape[0] // planes
    split = (groups, pair_y) + tokens.shape[1:]
    home = (part,) + tokens.shape[1:]
    z = lax.axis_index("z")
    held = {}
    for m in [*range(planes // 2, planes), *range(planes // 2 - 1, -1, -1)]:
        held[m] = lax.dynamic_slice_in_dim(tokens, (z ^ m) * part, part, 0)
        z, held[m] = lax.optimization_barrier((z, held[m]))
    at_whole = [in_plane(over_z(held[m], m)).reshape(split) for m in range(planes)]
    sent = open_side(tokens, cotangent, gate_weight, first_factor, planes)
    sent_whole = [over_z(in_plane(sent[m]), m).reshape(split) for m in range(planes)]
    *forward, mixed = forward_side(at_whole, last_factor, middle_factor)
    forward_home = [over_z(in_plane(forward[m].reshape(home)), m) for m in range(planes)]
    *backward, last_part, middle_part = backward_side(
        sent_whole, at_whole, mixed, last_factor.transpose(0, 2, 1), middle_factor
    )
    back_home = [over_z(in_plane(backward[m].reshape(home)), m) for m in range(planes)]
    gate_term, gate_part, first_part = close_side(
        tokens, cotangent, forward_home, gate_weight, first_factor
    )
    sums = reduced_direct(
        gate_part, first_part, middle_part, last_part, 1.0 / math.sqrt(positions(tokens, PLANES))
    )
    d_tokens = None
    for m in range(planes):
        d_tokens = finish(back_home[m], gate_term, m, d_tokens)
    return (d_tokens,) + sums


def direct(*arrays):
    return ordered(*arrays)


def fits(shape, groups, blocks):
    n_i, n_j, lanes, width = shape
    planes = blocks // 2
    return (
        n_i == groups * blocks
        and blocks == 2 * planes
        and planes & (planes - 1) == 0
        and n_i % (4 * planes) == 0
        and lanes % 16 == 0
        and n_j % 2 == 0
        and width == groups * 128
        and HEADS % groups == 0
        and width % (HEADS * 128) == 0
    )


def shards_of(mesh, tokens):
    groups, blocks = mesh.shape["grp"], mesh.shape["seq"]
    n_i, n_j, n_k, width = tokens.shape
    if fits((n_i, n_j // groups, n_k // blocks, width), groups, blocks):
        devices = mesh.devices.reshape(groups, blocks // 2, 2)
        return direct, jax.sharding.Mesh(devices, ("grp",) + PLANES), PLANES
    return general, mesh, "seq"


def solution(mesh):
    def step(*arrays):
        body, fine, seq = shards_of(mesh, arrays[0])
        spread_in = P(None, "grp", seq, None)
        in_specs = (spread_in, spread_in, P(), P(), P(), P())
        out_specs = (spread_in, P(seq, None), P(), P(None, "grp", None), P(None, seq, None))
        return jax.shard_map(body, mesh=fine, in_specs=in_specs, out_specs=out_specs, check_vma=False)(*arrays)

    return step
```
